32 devices in a mesh: seq: 8 (over y, x, core), head: 4 (over z).
Axes of the slice: x: 2, y: 2, z: 4, core: 2. Of those that a mesh axis runs over, the one named last changes fastest.
Arguments:
- queries: bfloat16 [4096, 4096], P('seq', 'head'), may hold values from -8 to 8
- keys: bfloat16 [4096, 4096], P('seq', 'head'), may hold values from -8 to 8
- values: bfloat16 [4096, 4096], P('seq', 'head'), may hold values from -6 to 6
- grad_normed: bfloat16 [4096, 4096], P('seq', 'head'), may hold values from -6 to 6
- docs: int32 [4096], P('seq'), may hold values from 0 to 3, as said below
Outputs:
- normed: bfloat16 [4096, 4096], P('seq', 'head')
- grad_queries: bfloat16 [4096, 4096], P('seq', 'head')
- grad_keys: bfloat16 [4096, 4096], P('seq', 'head')
- grad_values: bfloat16 [4096, 4096], P('seq', 'head')
The draws below stay inside these ranges and needn't reach their ends.
Inputs may be any that keep to these rules, and one draw needn't show every extreme that they name: docs never falls along the sequence; each of the 4 documents is a run of 1 to 3072 tokens, one of exactly 3072.
All inputs are finite; a program needn't handle non-finite values.
Results may differ from the reference program's by a relative error of at most 0.01.
Values may be sent and summed in bfloat16 or wider, within the bound.
No kernel may reach another device: no remote copies, remote signals or barrier semaphores. Data moves between devices by JAX's collectives and lax.ppermute only.
A program may use at most 192 MiB of HBM per device.

```python
import jax
import jax.numpy as jnp
from jax import lax

HEADS = 32
HEAD_DIM = 128
BLOCK = 512
SEQLEN = 4096
MOST_DOC = 3072
LEVELS = 3


def paired_fields(key):
    width = HEADS * HEAD_DIM
    query_key = jax.random.fold_in(key, 11)
    keys_key = jax.random.fold_in(key, 12)
    queries_out = jnp.clip(jax.random.normal(query_key, (SEQLEN, width), jnp.float32), -8.0, 8.0)
    keys_out = jnp.clip(jax.random.normal(keys_key, (SEQLEN, width), jnp.float32), -8.0, 8.0)
    return (queries_out, keys_out)


def draw_queries(key, part):
    return paired_fields(key)[0].astype(jnp.bfloat16)


def draw_keys(key, part):
    return paired_fields(key)[1].astype(jnp.bfloat16)


def draw_docs(key, part):
    rest = SEQLEN - MOST_DOC
    first_cut = jax.random.randint(jax.random.fold_in(key, 21), (), 1, rest - 1)
    second_cut = first_cut + jax.random.randint(jax.random.fold_in(key, 22), (), 1, rest - first_cut)
    long_slot = jax.random.randint(jax.random.fold_in(key, 23), (), 0, 4)
    short_lengths = jnp.stack([first_cut, second_cut - first_cut, rest - second_cut]).astype(jnp.int32)
    slots = jnp.arange(4, dtype=jnp.int32)
    short_index = jnp.clip(slots - (slots > long_slot).astype(jnp.int32), 0, 2)
    short_pick = jnp.sum(jnp.where(short_index[:, None] == jnp.arange(3, dtype=jnp.int32)[None, :], short_lengths[None, :], 0), axis=1)
    lengths = jnp.where(slots == long_slot, MOST_DOC, short_pick).astype(jnp.int32)
    bounds = jnp.cumsum(lengths)[:3]
    positions = jnp.arange(SEQLEN, dtype=jnp.int32)
    return jnp.sum((positions[:, None] >= bounds[None, :]).astype(jnp.int32), axis=1).astype(jnp.int32)


def block_levels(key, dims, shards, least, high):
    gain = 1.0
    for position, blocks in shards:
        draws = jax.random.uniform(jax.random.fold_in(jax.random.fold_in(key, 6), position), (blocks,), jnp.float32, least / len(shards), high / len(shards))
        gain = gain * jnp.repeat(jnp.exp(draws), dims[position] // blocks).reshape((-1,) + (1,) * (len(dims) - 1 - position))
    return gain


def bell_draw(own_key, dims, scale, limit, shards=(), kind=jnp.bfloat16):
    drawn = scale * jax.random.normal(own_key, dims, jnp.float32)
    if shards:
        drawn = drawn * block_levels(own_key, dims, shards, -0.22, 0.18)
    return jnp.clip(drawn, -limit, limit).astype(kind)


def setup_inputs(seed: int = 0) -> dict:
    arg_keys = jax.random.split(jax.random.key(seed), 6)
    queries = draw_queries(jax.random.fold_in(arg_keys[5], 71), 0)
    keys = draw_keys(jax.random.fold_in(arg_keys[5], 71), 0)
    values = bell_draw(arg_keys[2], (SEQLEN, HEADS * HEAD_DIM), 1.0, 6.0, ((0, 8), (1, 4)))
    grad_normed = bell_draw(arg_keys[3], (SEQLEN, HEADS * HEAD_DIM), 1.0, 6.0, ((0, 8), (1, 4)))
    docs = draw_docs(jax.random.fold_in(arg_keys[5], 71), 0)
    return dict(queries=queries, keys=keys, values=values, grad_normed=grad_normed, docs=docs)


norm_eps = 1e-06

def reference(queries, keys, values, grad_normed, docs):
    width = HEADS * HEAD_DIM
    num_blocks = SEQLEN // BLOCK
    offsets = [0] + [2 ** exponent for exponent in range(LEVELS)]
    score_scale = 1.0 / HEAD_DIM ** 0.5
    arange_block = jnp.arange(BLOCK, dtype=jnp.int32)

    def one_block(grad_store, query_block):
        query_start = query_block * BLOCK
        query_pos = query_start + arange_block
        query_docs = lax.dynamic_slice_in_dim(docs, query_start, BLOCK)
        query_rows = lax.dynamic_slice_in_dim(queries, query_start, BLOCK).astype(jnp.float32).reshape(BLOCK, HEADS, HEAD_DIM)
        cotangent = lax.dynamic_slice_in_dim(grad_normed, query_start, BLOCK).astype(jnp.float32)
        starts = []
        key_list = []
        value_list = []
        mask_list = []
        for offset in offsets:
            key_start = (query_block - offset) * BLOCK
            safe_start = jnp.maximum(key_start, 0).astype(jnp.int32)
            key_pos = key_start + arange_block
            key_docs = lax.dynamic_slice_in_dim(docs, safe_start, BLOCK)
            allowed = (key_pos[None, :] >= 0) & (key_pos[None, :] <= query_pos[:, None]) & (key_docs[None, :] == query_docs[:, None])
            starts.append(safe_start)
            key_list.append(lax.dynamic_slice_in_dim(keys, safe_start, BLOCK))
            value_list.append(lax.dynamic_slice_in_dim(values, safe_start, BLOCK))
            mask_list.append(allowed)
        key_rows = jnp.stack(key_list).astype(jnp.float32).reshape(len(offsets), BLOCK, HEADS, HEAD_DIM)
        value_rows = jnp.stack(value_list).astype(jnp.float32).reshape(len(offsets), BLOCK, HEADS, HEAD_DIM)
        masks = jnp.stack(mask_list)
        scores = jnp.einsum('qhd,nkhd->nhqk', query_rows, key_rows) * score_scale
        scores = jnp.where(masks[:, None], scores, -jnp.inf)
        row_max = lax.optimization_barrier(jnp.max(scores, axis=(0, 3)))
        row_sum = lax.optimization_barrier(jnp.sum(jnp.exp(scores - row_max[None, :, :, None]), axis=(0, 3)))
        log_total = row_max + jnp.log(row_sum)
        prob_exact = jnp.exp(scores - log_total[None, :, :, None])
        prob_round = prob_exact.astype(jnp.bfloat16)
        attn = jnp.einsum('nhqk,nkhd->qhd', prob_round.astype(jnp.float32), value_rows)
        attn_flat = attn.reshape(BLOCK, width)
        inv_rms = lax.rsqrt(lax.optimization_barrier(jnp.sum(attn_flat * attn_flat, axis=-1)) / width + norm_eps)
        normed = (attn_flat * inv_rms[:, None]).astype(jnp.bfloat16)
        projection = lax.optimization_barrier(jnp.sum(cotangent * attn_flat, axis=-1))
        dattn = (inv_rms[:, None] * cotangent - attn_flat * (inv_rms ** 3 * projection / width)[:, None]).astype(jnp.bfloat16)
        dattn_heads = dattn.astype(jnp.float32).reshape(BLOCK, HEADS, HEAD_DIM)
        row_delta = lax.optimization_barrier(jnp.sum(dattn_heads * attn, axis=-1)).T
        dprob = jnp.einsum('qhd,nkhd->nhqk', dattn_heads, value_rows)
        dscore = (prob_exact * (dprob - row_delta[None, :, :, None]) * score_scale).astype(jnp.bfloat16).astype(jnp.float32)
        grad_query = jnp.einsum('nhqk,nkhd->qhd', dscore, key_rows).reshape(BLOCK, width).astype(jnp.bfloat16)
        key_terms = jnp.einsum('nhqk,qhd->nkhd', dscore, query_rows).reshape(len(offsets), BLOCK, width)
        value_terms = jnp.einsum('nhqk,qhd->nkhd', prob_round.astype(jnp.float32), dattn_heads).reshape(len(offsets), BLOCK, width)
        for number in range(len(offsets)):
            current = lax.dynamic_slice_in_dim(grad_store, starts[number], BLOCK, axis=1)
            update = jnp.stack([key_terms[number], value_terms[number]])
            grad_store = lax.dynamic_update_slice_in_dim(grad_store, current + update, starts[number], axis=1)
        return (grad_store, (normed, grad_query))
    grad_store = jnp.zeros((2, SEQLEN, width), jnp.float32)
    grad_store, outputs = lax.scan(one_block, grad_store, jnp.arange(num_blocks, dtype=jnp.int32))
    normed = outputs[0].reshape(SEQLEN, width)
    grad_queries = outputs[1].reshape(SEQLEN, width)
    return (normed, grad_queries, grad_store[0].astype(jnp.bfloat16), grad_store[1].astype(jnp.bfloat16))
```

```python
import functools
import math

import jax
import jax.numpy as jnp
from jax import lax
from jax.experimental import pallas as pl
from jax.experimental.pallas import tpu as pltpu
from jax.sharding import PartitionSpec as P

HEADS = 32
HEAD_DIM = 128


norm_eps = 1e-06

OFFSETS = (0, 1, 2, 4)
NEG = -1e30
F32 = jnp.float32
BF16 = jnp.bfloat16
VMEM_BYTES = 60 * 1024 * 1024


def copy_in(rank, refs, held, sems):
    copies = [
        pltpu.make_async_copy(ref, held.at[rank ^ m], sems.at[m]) for m, ref in enumerate(refs)
    ]
    for copy in copies:
        copy.start()
    for copy in copies:
        copy.wait()


def find_bounds(held, block, bounds):
    ids = held[:, 3 * block :, :].astype(F32)
    for d in range(3):
        count = jnp.sum(jnp.where(ids < d + 0.5, 1.0, 0.0))
        bounds[d] = count.astype(jnp.int32)


def doc_of(position, bounds):
    doc = jnp.int32(0)
    for d in range(3):
        doc = doc + (position >= bounds[d]).astype(jnp.int32)
    return doc


def pair_state(i, off, block, bounds):
    j = jnp.maximum(i - off, 0)
    if off == 0:
        return j, None, None
    active = (i >= off) & (doc_of(i * block, bounds) == doc_of(j * block + block - 1, bounds))
    full = doc_of(j * block, bounds) == doc_of(i * block + block - 1, bounds)
    return j, active, full


def doc_starts(i, block, bounds):
    pos = i * block + lax.broadcasted_iota(jnp.int32, (1, block), 1)
    start = jnp.zeros((1, block), jnp.int32)
    for d in range(3):
        start = jnp.where(pos >= bounds[d], jnp.maximum(start, bounds[d]), start)
    return pos, start


def nt_dot(a, b):
    return lax.dot_general(a, b, (((1,), (1,)), ((), ())), preferred_element_type=F32)


def nn_dot(a, b):
    return lax.dot_general(a, b, (((1,), (0,)), ((), ())), preferred_element_type=F32)


def forward_kernel(block, rank_ref, *refs):
    n = 8
    a_refs = refs[:n]
    prob_ref, out_t_ref, out_ref, inv_ref, square_ref = refs[n : n + 5]
    held, val_t, score, top, total, acc, bounds, sems = refs[n + 5 :]
    i = pl.program_id(0)

    @pl.when(i == 0)
    def _():
        copy_in(rank_ref[0], a_refs, held, sems)
        find_bounds(held, block, bounds)
        for t in range(n):
            val_t[t] = held[t, 2 * block : 3 * block, :].T

    gain = math.log2(math.e) / math.sqrt(HEAD_DIM)
    query = held[i, 0:block, :]
    q_pos, q_start = doc_starts(i, block, bounds)
    pairs = [(off,) + pair_state(i, off, block, bounds) for off in OFFSETS]

    def put_score(slot, off, j, masked):
        s = nt_dot(held[j, block : 2 * block, :], query) * gain
        if masked:
            k_pos = j * block + lax.broadcasted_iota(jnp.int32, (block, 1), 0)
            keep = k_pos >= q_start
            if off == 0:
                keep = keep & (k_pos <= q_pos)
            s = jnp.where(keep, s, NEG)
        score[slot] = s
        peak = jnp.max(s, axis=0, keepdims=True)
        top[...] = peak if off == 0 else jnp.maximum(top[...], peak)

    for slot, (off, j, active, full) in enumerate(pairs):
        if off == 0:
            put_score(slot, off, j, True)
        else:
            pl.when(active & full)(functools.partial(put_score, slot, off, j, False))
            pl.when(active & jnp.logical_not(full))(functools.partial(put_score, slot, off, j, True))

    def take_probs(slot, off, j):
        p = jnp.exp2(score[slot] - top[...])
        row = jnp.sum(p, axis=0, keepdims=True)
        pb = p.astype(BF16)
        prob_ref[0, slot] = pb
        term = nn_dot(val_t[j], pb)
        if off == 0:
            total[...] = row
            acc[...] = term
        else:
            total[...] += row
            acc[...] += term

    for slot, (off, j, active, full) in enumerate(pairs):
        if off == 0:
            take_probs(slot, off, j)
        else:
            pl.when(active)(functools.partial(take_probs, slot, off, j))

    inv = 1.0 / total[...]
    out_t = acc[...] * inv
    out_t_ref[0] = out_t
    out_ref[0] = out_t.T.astype(BF16)
    inv_ref[0] = inv
    square_ref[0] = jnp.sum(out_t * out_t, axis=0, keepdims=True)


def project_kernel(block, rank_ref, *refs):
    n = 8
    g_refs = refs[:n]
    out_t_ref, square_ref, stats_ref, held, sems = refs[n:]
    copy_in(rank_ref[0], g_refs, held, sems)
    for t in range(n):
        cot_t = held[t].astype(F32).T
        cols = slice(t * block, (t + 1) * block)
        stats_ref[0:1, cols] = square_ref[t]
        stats_ref[1:2, cols] = jnp.sum(cot_t * out_t_ref[t], axis=0, keepdims=True)


def backward_kernel(block, rank_ref, *refs):
    n = 8
    a_refs, g_refs = refs[:n], refs[n : 2 * n]
    prob_ref, out_t_ref, inv_ref, stats_ref = refs[2 * n : 2 * n + 4]
    d_refs = refs[2 * n + 4 : 3 * n + 4]
    held, cot, key_t, grad_q, grad_k, grad_v, acc, bounds, sems, sems_g = refs[3 * n + 4 :]
    i = pl.program_id(0)
    scale = 1.0 / math.sqrt(HEAD_DIM)
    width = HEADS * HEAD_DIM

    @pl.when(i == 0)
    def _():
        copies = [
            pltpu.make_async_copy(ref, cot.at[rank_ref[0] ^ m], sems_g.at[m])
            for m, ref in enumerate(g_refs)
        ]
        for copy in copies:
            copy.start()
        copy_in(rank_ref[0], a_refs, held, sems)
        for copy in copies:
            copy.wait()
        find_bounds(held, block, bounds)
        for t in range(n):
            key_t[t] = held[t, block : 2 * block, :].T
        grad_k[...] = jnp.zeros_like(grad_k)
        grad_v[...] = jnp.zeros_like(grad_v)

    inv_rms = lax.rsqrt(stats_ref[0, 0:1, :] / width + norm_eps)
    coef = inv_rms * inv_rms * inv_rms * stats_ref[0, 1:2, :] / width
    out_t = out_t_ref[0]
    dattn_t = (inv_rms * cot[i].astype(F32).T - out_t * coef) * inv_ref[0]
    dattn_tb = dattn_t.astype(BF16)
    dattn_f = dattn_tb.astype(F32)
    delta = jnp.sum(dattn_f * out_t, axis=0, keepdims=True)
    dattn = dattn_f.T.astype(BF16)
    query = held[i, 0:block, :]

    def one_pair(slot, off, j):
        pb = prob_ref[0, slot]
        dprob = nn_dot(held[j, 2 * block : 3 * block, :], dattn_tb)
        ds = (pb.astype(F32) * (dprob - delta)).astype(BF16)
        term = nn_dot(key_t[j], ds)
        if off == 0:
            acc[...] = term
        else:
            acc[...] += term
        grad_k[j] += nn_dot(ds, query)
        grad_v[j] += nn_dot(pb, dattn)

    for slot, off in enumerate(OFFSETS):
        j, active, full = pair_state(i, off, block, bounds)
        if off == 0:
            one_pair(slot, off, j)
        else:
            pl.when(active)(functools.partial(one_pair, slot, off, j))

    grad_q[i] = (acc[...] * scale).T.astype(BF16)

    @pl.when(i == n - 1)
    def _():
        for m in range(n):
            t = rank_ref[0] ^ m
            d_refs[m][0:block, :] = grad_q[t]
            d_refs[m][block : 2 * block, :] = (grad_k[t] * scale).astype(BF16)
            d_refs[m][2 * block :, :] = grad_v[t].astype(BF16)


def pack_kernel(block, rank_ref, q_ref, k_ref, v_ref, g_ref, doc_ref, *refs):
    n = 8
    a_refs, g_refs, sems = refs[:n], refs[n : 2 * n], refs[2 * n]
    copies = []
    for m in range(n):
        cols = pl.ds(pl.multiple_of((rank_ref[0] ^ m) * HEAD_DIM, HEAD_DIM), HEAD_DIM)
        parts = [
            (q_ref.at[:, cols], a_refs[m].at[0:block, :]),
            (k_ref.at[:, cols], a_refs[m].at[block : 2 * block, :]),
            (v_ref.at[:, cols], a_refs[m].at[2 * block : 3 * block, :]),
            (doc_ref, a_refs[m].at[3 * block :, :]),
            (g_ref.at[:, cols], g_refs[m]),
        ]
        for source, target in parts:
            copies.append(pltpu.make_async_copy(source, target, sems.at[len(copies)]))
    for copy in copies:
        copy.start()
    for copy in copies:
        copy.wait()


def unpack_kernel(block, rank_ref, *refs):
    n = 8
    d_refs, outs, sems = refs[:n], refs[n : n + 3], refs[n + 3]
    copies = []
    for m in range(n):
        cols = pl.ds(pl.multiple_of((rank_ref[0] ^ m) * HEAD_DIM, HEAD_DIM), HEAD_DIM)
        for part, out in enumerate(outs):
            rows = slice(part * block, (part + 1) * block)
            copies.append(
                pltpu.make_async_copy(d_refs[m].at[rows, :], out.at[:, cols], sems.at[len(copies)])
            )
    for copy in copies:
        copy.start()
    for copy in copies:
        copy.wait()


def normed_kernel(block, rank_ref, stats_ref, *refs):
    n = 8
    o_refs, out_ref = refs[:n], refs[n]
    inv_rms = lax.rsqrt(stats_ref[0, 0:1, :] / (HEADS * HEAD_DIM) + norm_eps)
    spread = jnp.broadcast_to(inv_rms, (HEAD_DIM, block)).T
    for m in range(n):
        cols = pl.ds(pl.multiple_of((rank_ref[0] ^ m) * HEAD_DIM, HEAD_DIM), HEAD_DIM)
        out_ref[:, cols] = (o_refs[m][...].astype(F32) * spread).astype(BF16)


SMEM_SPEC = pl.BlockSpec(memory_space=pltpu.SMEM)
ANY_SPEC = pl.BlockSpec(memory_space=pl.ANY)
VMEM_SPEC = pl.BlockSpec(memory_space=pltpu.VMEM)


def shape_of(shape, dtype):
    return jax.ShapeDtypeStruct(shape, dtype)


def swap(value, m):
    if m == 0:
        return value
    n = lax.axis_size("seq")
    return lax.ppermute(value, "seq", [(s, s ^ m) for s in range(n)])


def sum_everywhere(stats):
    stats = stats + swap(stats, 1)
    stats = stats + swap(stats, 2) + swap(stats, 4) + swap(stats, 6)
    heads = lax.axis_size("head")
    parts = [
        lax.ppermute(stats, "head", [(s, (s + d) % heads) for s in range(heads)])
        for d in range(1, heads)
    ]
    return functools.reduce(jnp.add, parts, stats)


def by_head(queries, keys, values, grad_normed, docs):
    block, width_dev = queries.shape
    n = width_dev // HEAD_DIM
    rank = lax.axis_index("seq").reshape(1).astype(jnp.int32)
    doc_rows = jnp.pad(
        docs.astype(BF16).reshape(block // 128, 128), ((0, 16 - block // 128), (0, 0)),
        constant_values=4.0,
    )
    rows = 3 * block + 16
    params = pltpu.CompilerParams(vmem_limit_bytes=VMEM_BYTES)
    packed = pl.pallas_call(
        functools.partial(pack_kernel, block),
        out_shape=[shape_of((rows, HEAD_DIM), BF16)] * n + [shape_of((block, HEAD_DIM), BF16)] * n,
        in_specs=[SMEM_SPEC] + [ANY_SPEC] * 5,
        out_specs=[ANY_SPEC] * (2 * n),
        scratch_shapes=[pltpu.SemaphoreType.DMA((5 * n,))],
        name="pack",
    )(rank, queries, keys, values, grad_normed, doc_rows)
    a = [swap(packed[m], m) for m in range(n)]
    g = [swap(packed[n + m], m) for m in range(n)]

    step = lambda *shape: pl.BlockSpec((1,) + shape, lambda i: (i,) + (0,) * len(shape))
    probs, out_t, out, inv_total, square = pl.pallas_call(
        functools.partial(forward_kernel, block),
        grid=(n,),
        out_shape=[
            shape_of((n, len(OFFSETS), block, block), BF16),
            shape_of((n, HEAD_DIM, block), F32),
            shape_of((n, block, HEAD_DIM), BF16),
            shape_of((n, 1, block), F32),
            shape_of((n, 1, block), F32),
        ],
        in_specs=[SMEM_SPEC] + [ANY_SPEC] * n,
        out_specs=[
            step(len(OFFSETS), block, block),
            step(HEAD_DIM, block),
            step(block, HEAD_DIM),
            step(1, block),
            step(1, block),
        ],
        scratch_shapes=[
            pltpu.VMEM((n, rows, HEAD_DIM), BF16),
            pltpu.VMEM((n, HEAD_DIM, block), BF16),
            pltpu.VMEM((len(OFFSETS), block, block), F32),
            pltpu.VMEM((1, block), F32),
            pltpu.VMEM((1, block), F32),
            pltpu.VMEM((HEAD_DIM, block), F32),
            pltpu.SMEM((3,), jnp.int32),
            pltpu.SemaphoreType.DMA((n,)),
        ],
        compiler_params=params,
        name="forward",
    )(rank, *a)

    stats = pl.pallas_call(
        functools.partial(project_kernel, block),
        out_shape=shape_of((2, n * block), F32),
        in_specs=[SMEM_SPEC] + [ANY_SPEC] * n + [VMEM_SPEC] * 2,
        out_specs=VMEM_SPEC,
        scratch_shapes=[
            pltpu.VMEM((n, block, HEAD_DIM), BF16),
            pltpu.SemaphoreType.DMA((n,)),
        ],
        compiler_params=params,
        name="project",
    )(rank, *g, out_t, square)
    stats = sum_everywhere(stats)

    home = [
        swap(lax.dynamic_index_in_dim(out, rank[0] ^ m, 0, keepdims=False), m) for m in range(n)
    ]
    stats_by_block = stats.reshape(2, n, block).transpose(1, 0, 2)
    own_stats = lax.dynamic_slice_in_dim(stats_by_block, rank[0], 1, axis=0)
    normed = pl.pallas_call(
        functools.partial(normed_kernel, block),
        out_shape=shape_of((block, width_dev), BF16),
        in_specs=[SMEM_SPEC] + [VMEM_SPEC] * (n + 1),
        out_specs=VMEM_SPEC,
        compiler_params=params,
        name="normed",
    )(rank, own_stats, *home)

    grads = pl.pallas_call(
        functools.partial(backward_kernel, block),
        grid=(n,),
        out_shape=[shape_of((3 * block, HEAD_DIM), BF16)] * n,
        in_specs=[SMEM_SPEC] + [ANY_SPEC] * (2 * n) + [
            step(len(OFFSETS), block, block),
            step(HEAD_DIM, block),
            step(1, block),
            step(2, block),
        ],
        out_specs=[pl.BlockSpec((3 * block, HEAD_DIM), lambda i: (0, 0))] * n,
        scratch_shapes=[
            pltpu.VMEM((n, rows, HEAD_DIM), BF16),
            pltpu.VMEM((n, block, HEAD_DIM), BF16),
            pltpu.VMEM((n, HEAD_DIM, block), BF16),
            pltpu.VMEM((n, block, HEAD_DIM), BF16),
            pltpu.VMEM((n, block, HEAD_DIM), F32),
            pltpu.VMEM((n, block, HEAD_DIM), F32),
            pltpu.VMEM((HEAD_DIM, block), F32),
            pltpu.SMEM((3,), jnp.int32),
            pltpu.SemaphoreType.DMA((n,)),
            pltpu.SemaphoreType.DMA((n,)),
        ],
        compiler_params=params,
        name="backward",
    )(rank, *a, *g, probs, out_t, inv_total, stats_by_block)
    back = [swap(grads[m], m) for m in range(n)]
    grad_outs = pl.pallas_call(
        functools.partial(unpack_kernel, block),
        out_shape=[shape_of((block, width_dev), BF16)] * 3,
        in_specs=[SMEM_SPEC] + [ANY_SPEC] * n,
        out_specs=[ANY_SPEC] * 3,
        scratch_shapes=[pltpu.SemaphoreType.DMA((3 * n,))],
        name="unpack",
    )(rank, *back)
    return (normed, *grad_outs)


def from_behind(value, axis, steps):
    count = lax.axis_size(axis)
    initial, last = (max(0, -steps), min(count, count - steps))
    return lax.ppermute(value, axis, [(source, source + steps) for source in range(initial, last)])


def allowed_pairs(all_docs, own_docs, query_pos, seq_rank, offset, block_len):
    key_start = (seq_rank - offset) * block_len
    key_pos = key_start + jnp.arange(block_len, dtype=jnp.int32)
    key_docs = lax.dynamic_slice_in_dim(all_docs, jnp.maximum(key_start, 0), block_len)
    return (
        (key_pos[None, :] >= 0)
        & (key_pos[None, :] <= query_pos[:, None])
        & (key_docs[None, :] == own_docs[:, None])
    )


def masked_scores(query_heads, source, allowed, score_scale):
    key_heads = source[0].reshape(query_heads.shape)
    scores = (
        jnp.einsum("qhd,khd->hqk", query_heads, key_heads, preferred_element_type=jnp.float32)
        * score_scale
    )
    return jnp.where(allowed[None], scores, -jnp.inf)


def by_block(queries, keys, values, grad_normed, docs):
    block_len, width_dev = queries.shape
    heads_dev = width_dev // HEAD_DIM
    width = HEADS * HEAD_DIM
    score_scale = 1.0 / math.sqrt(HEAD_DIM)
    seq_rank = lax.axis_index("seq")
    levels = lax.axis_size("seq").bit_length() - 1
    distances = [2**exponent for exponent in range(levels)]
    all_docs = lax.all_gather(docs, "seq", axis=0, tiled=True)
    query_pos = seq_rank * block_len + jnp.arange(block_len, dtype=jnp.int32)
    query_heads = queries.reshape(block_len, heads_dev, HEAD_DIM)
    key_value = jnp.stack([keys, values])
    fetched = [from_behind(key_value, "seq", offset) for offset in distances]
    offsets = [0] + distances
    sources = [key_value] + fetched
    masks = [
        allowed_pairs(all_docs, docs, query_pos, seq_rank, offset, block_len) for offset in offsets
    ]
    shape_heads = (block_len, heads_dev, HEAD_DIM)
    row_max = jnp.full((heads_dev, block_len), -jnp.inf, jnp.float32)
    row_sum = jnp.zeros((heads_dev, block_len), jnp.float32)
    for source, allowed in zip(sources, masks):

        def update_stats(state, source_kv, allowed_now):
            old_max, old_sum = state
            scores = masked_scores(query_heads, source_kv, allowed_now, score_scale)
            new_max = jnp.maximum(old_max, jnp.max(scores, axis=-1))
            new_sum = old_sum * jnp.exp(old_max - new_max) + jnp.sum(
                jnp.exp(scores - new_max[..., None]), axis=-1
            )
            return (new_max, new_sum)

        def keep_stats(state, source_kv, allowed_now):
            return state

        row_max, row_sum = lax.cond(
            jnp.any(allowed), update_stats, keep_stats, (row_max, row_sum), source, allowed
        )
    log_total = row_max + jnp.log(row_sum)
    attn = jnp.zeros(shape_heads, jnp.float32)
    for source, allowed in zip(sources, masks):

        def forward_term(source_kv, allowed_now):
            scores = masked_scores(query_heads, source_kv, allowed_now, score_scale)
            prob_round = jnp.exp(scores - log_total[..., None]).astype(jnp.bfloat16)
            value_heads = source_kv[1].reshape(shape_heads)
            return jnp.einsum(
                "hqk,khd->qhd", prob_round, value_heads, preferred_element_type=jnp.float32
            )

        def empty_term(source_kv, allowed_now):
            return jnp.zeros(shape_heads, jnp.float32)

        attn = attn + lax.cond(jnp.any(allowed), forward_term, empty_term, source, allowed)
    attn_flat = attn.reshape(block_len, width_dev)
    cotangent = grad_normed.astype(jnp.float32)
    square_local = jnp.sum(attn_flat * attn_flat, axis=-1)
    square_total = lax.psum(square_local, "head")
    inv_rms = lax.rsqrt(square_total / width + norm_eps)
    normed = (attn_flat * inv_rms[:, None]).astype(jnp.bfloat16)
    projection = lax.psum(jnp.sum(cotangent * attn_flat, axis=-1), "head")
    dattn = (
        inv_rms[:, None] * cotangent - attn_flat * (inv_rms**3 * projection / width)[:, None]
    ).astype(jnp.bfloat16)
    dattn_heads = dattn.reshape(shape_heads)
    row_delta = jnp.sum(dattn_heads.astype(jnp.float32) * attn, axis=-1).T
    grad_query = jnp.zeros(shape_heads, jnp.float32)
    partials = []
    for source, allowed in zip(sources, masks):

        def backward_term(source_kv, allowed_now):
            scores = masked_scores(query_heads, source_kv, allowed_now, score_scale)
            prob_exact = jnp.exp(scores - log_total[..., None])
            prob_round = prob_exact.astype(jnp.bfloat16)
            key_heads = source_kv[0].reshape(shape_heads)
            value_heads = source_kv[1].reshape(shape_heads)
            dprob = jnp.einsum(
                "qhd,khd->hqk", dattn_heads, value_heads, preferred_element_type=jnp.float32
            )
            dscore = (prob_exact * (dprob - row_delta[..., None]) * score_scale).astype(
                jnp.bfloat16
            )
            query_term = jnp.einsum(
                "hqk,khd->qhd", dscore, key_heads, preferred_element_type=jnp.float32
            )
            key_term = jnp.einsum(
                "hqk,qhd->khd", dscore, query_heads, preferred_element_type=jnp.float32
            )
            value_term = jnp.einsum(
                "hqk,qhd->khd", prob_round, dattn_heads, preferred_element_type=jnp.float32
            )
            return (
                query_term,
                jnp.stack(
                    [
                        key_term.reshape(block_len, width_dev),
                        value_term.reshape(block_len, width_dev),
                    ]
                ),
            )

        def empty_pair(source_kv, allowed_now):
            return (
                jnp.zeros(shape_heads, jnp.float32),
                jnp.zeros((2, block_len, width_dev), jnp.float32),
            )

        query_term, pair_term = lax.cond(
            jnp.any(allowed), backward_term, empty_pair, source, allowed
        )
        grad_query = grad_query + query_term
        partials.append(pair_term)
    local_term = partials[0]
    far_terms = partials[1:]
    summed = local_term
    for offset, addend in zip(distances, far_terms):
        summed = summed + from_behind(addend.astype(jnp.bfloat16), "seq", -offset).astype(
            addend.dtype
        )
    grad_queries = grad_query.reshape(block_len, width_dev).astype(jnp.bfloat16)
    return (normed, grad_queries, summed[0].astype(jnp.bfloat16), summed[1].astype(jnp.bfloat16))


def body(queries, *others):
    block_len, width_dev = queries.shape
    if lax.axis_size("seq") == 8 and width_dev == 8 * HEAD_DIM and block_len == 512:
        return by_head(queries, *others)
    return by_block(queries, *others)


def solution(mesh):
    placed = (P("seq", "head"), P("seq", "head"), P("seq", "head"), P("seq", "head"), P("seq"))
    return jax.shard_map(
        body,
        mesh=mesh,
        in_specs=placed,
        out_specs=(P("seq", "head"), P("seq", "head"), P("seq", "head"), P("seq", "head")),
        check_vma=False,
    )
```

```python
import functools
import math

import jax
import jax.numpy as jnp
from jax import lax
from jax.experimental import pallas as pl
from jax.experimental.pallas import tpu as pltpu
from jax.sharding import PartitionSpec as P

HEADS = 32
HEAD_DIM = 128


norm_eps = 1e-06

OFFSETS = (0, 1, 2, 4)
NEG = -1e30
F32 = jnp.float32
BF16 = jnp.bfloat16
VMEM_BYTES = 60 * 1024 * 1024


def copy_in(rank, refs, held, sems):
    copies = [
        pltpu.make_async_copy(ref, held.at[rank ^ m], sems.at[m]) for m, ref in enumerate(refs)
    ]
    for copy in copies:
        copy.start()
    for copy in copies:
        copy.wait()


def find_bounds(held, block, bounds):
    ids = held[:, 3 * block :, :].astype(F32)
    for d in range(3):
        count = jnp.sum(jnp.where(ids < d + 0.5, 1.0, 0.0))
        bounds[d] = count.astype(jnp.int32)


def doc_of(position, bounds):
    doc = jnp.int32(0)
    for d in range(3):
        doc = doc + (position >= bounds[d]).astype(jnp.int32)
    return doc


def pair_state(i, off, block, bounds):
    j = jnp.maximum(i - off, 0)
    if off == 0:
        return j, None, None
    active = (i >= off) & (doc_of(i * block, bounds) == doc_of(j * block + block - 1, bounds))
    full = doc_of(j * block, bounds) == doc_of(i * block + block - 1, bounds)
    return j, active, full


def doc_starts(i, block, bounds):
    pos = i * block + lax.broadcasted_iota(jnp.int32, (1, block), 1)
    start = jnp.zeros((1, block), jnp.int32)
    for d in range(3):
        start = jnp.where(pos >= bounds[d], jnp.maximum(start, bounds[d]), start)
    return pos, start


def nt_dot(a, b):
    return lax.dot_general(a, b, (((1,), (1,)), ((), ())), preferred_element_type=F32)


def nn_dot(a, b):
    return lax.dot_general(a, b, (((1,), (0,)), ((), ())), preferred_element_type=F32)


def forward_kernel(block, rank_ref, *refs):
    n = 8
    a_refs = refs[:n]
    prob_ref, out_t_ref, out_ref, inv_ref, square_ref = refs[n : n + 5]
    held, val_t, score, top, total, acc, bounds, sems = refs[n + 5 :]
    i = pl.program_id(0)

    @pl.when(i == 0)
    def _():
        copy_in(rank_ref[0], a_refs, held, sems)
        find_bounds(held, block, bounds)
        for t in range(n):
            val_t[t] = held[t, 2 * block : 3 * block, :].T

    gain = math.log2(math.e) / math.sqrt(HEAD_DIM)
    query = held[i, 0:block, :]
    q_pos, q_start = doc_starts(i, block, bounds)
    pairs = [(off,) + pair_state(i, off, block, bounds) for off in OFFSETS]

    def put_score(slot, off, j, masked):
        s = nt_dot(held[j, block : 2 * block, :], query) * gain
        if masked:
            k_pos = j * block + lax.broadcasted_iota(jnp.int32, (block, 1), 0)
            keep = k_pos >= q_start
            if off == 0:
                keep = keep & (k_pos <= q_pos)
            s = jnp.where(keep, s, NEG)
        score[slot] = s
        peak = jnp.max(s, axis=0, keepdims=True)
        top[...] = peak if off == 0 else jnp.maximum(top[...], peak)

    for slot, (off, j, active, full) in enumerate(pairs):
        if off == 0:
            put_score(slot, off, j, True)
        else:
            pl.when(active & full)(functools.partial(put_score, slot, off, j, False))
            pl.when(active & jnp.logical_not(full))(functools.partial(put_score, slot, off, j, True))

    def take_probs(slot, off, j):
        p = jnp.exp2(score[slot] - top[...])
        row = jnp.sum(p, axis=0, keepdims=True)
        pb = p.astype(BF16)
        prob_ref[0, slot] = pb
        term = nn_dot(val_t[j], pb)
        if off == 0:
            total[...] = row
            acc[...] = term
        else:
            total[...] += row
            acc[...] += term

    for slot, (off, j, active, full) in enumerate(pairs):
        if off == 0:
            take_probs(slot, off, j)
        else:
            pl.when(active)(functools.partial(take_probs, slot, off, j))

    inv = 1.0 / total[...]
    out_t = acc[...] * inv
    out_t_ref[0] = out_t
    out_ref[0] = out_t.T.astype(BF16)
    inv_ref[0] = inv
    square_ref[0] = jnp.sum(out_t * out_t, axis=0, keepdims=True)


def project_kernel(block, rank_ref, *refs):
    n = 8
    g_refs = refs[:n]
    out_t_ref, square_ref, stats_ref, held, sems = refs[n:]
    copy_in(rank_ref[0], g_refs, held, sems)
    for t in range(n):
        cot_t = held[t].astype(F32).T
        cols = slice(t * block, (t + 1) * block)
        stats_ref[0:1, cols] = square_ref[t]
        stats_ref[1:2, cols] = jnp.sum(cot_t * out_t_ref[t], axis=0, keepdims=True)


def backward_kernel(block, rank_ref, *refs):
    n = 8
    a_refs, g_refs = refs[:n], refs[n : 2 * n]
    prob_ref, out_t_ref, inv_ref, stats_ref = refs[2 * n : 2 * n + 4]
    d_refs = refs[2 * n + 4 : 3 * n + 4]
    held, cot, key_t, grad_q, grad_k, grad_v, acc, bounds, sems, sems_g = refs[3 * n + 4 :]
    i = pl.program_id(0)
    scale = 1.0 / math.sqrt(HEAD_DIM)
    width = HEADS * HEAD_DIM

    @pl.when(i == 0)
    def _():
        copies = [
            pltpu.make_async_copy(ref, cot.at[rank_ref[0] ^ m], sems_g.at[m])
            for m, ref in enumerate(g_refs)
        ]
        for copy in copies:
            copy.start()
        copy_in(rank_ref[0], a_refs, held, sems)
        for copy in copies:
            copy.wait()
        find_bounds(held, block, bounds)
        for t in range(n):
            key_t[t] = held[t, block : 2 * block, :].T
        grad_k[...] = jnp.zeros_like(grad_k)
        grad_v[...] = jnp.zeros_like(grad_v)

    inv_rms = lax.rsqrt(stats_ref[0, 0:1, :] / width + norm_eps)
    coef = inv_rms * inv_rms * inv_rms * stats_ref[0, 1:2, :] / width
    out_t = out_t_ref[0]
    dattn_t = (inv_rms * cot[i].astype(F32).T - out_t * coef) * inv_ref[0]
    dattn_tb = dattn_t.astype(BF16)
    dattn_f = dattn_tb.astype(F32)
    delta = jnp.sum(dattn_f * out_t, axis=0, keepdims=True)
    dattn = dattn_f.T.astype(BF16)
    query = held[i, 0:block, :]

    def one_pair(slot, off, j):
        pb = prob_ref[0, slot]
        dprob = nn_dot(held[j, 2 * block : 3 * block, :], dattn_tb)
        ds = (pb.astype(F32) * (dprob - delta)).astype(BF16)
        term = nn_dot(key_t[j], ds)
        if off == 0:
            acc[...] = term
        else:
            acc[...] += term
        grad_k[j] += nn_dot(ds, query)
        grad_v[j] += nn_dot(pb, dattn)

    for slot, off in enumerate(OFFSETS):
        j, active, full = pair_state(i, off, block, bounds)
        if off == 0:
            one_pair(slot, off, j)
        else:
            pl.when(active)(functools.partial(one_pair, slot, off, j))

    grad_q[i] = (acc[...] * scale).T.astype(BF16)

    @pl.when(i == n - 1)
    def _():
        for m in range(n):
            t = rank_ref[0] ^ m
            d_refs[m][0:block, :] = grad_q[t]
            d_refs[m][block : 2 * block, :] = (grad_k[t] * scale).astype(BF16)
            d_refs[m][2 * block :, :] = grad_v[t].astype(BF16)


def pack_kernel(block, rank_ref, q_ref, k_ref, v_ref, g_ref, doc_ref, *refs):
    n = 8
    a_refs, g_refs, sems = refs[:n], refs[n : 2 * n], refs[2 * n]
    copies = []
    for m in range(n):
        cols = pl.ds(pl.multiple_of((rank_ref[0] ^ m) * HEAD_DIM, HEAD_DIM), HEAD_DIM)
        parts = [
            (q_ref.at[:, cols], a_refs[m].at[0:block, :]),
            (k_ref.at[:, cols], a_refs[m].at[block : 2 * block, :]),
            (v_ref.at[:, cols], a_refs[m].at[2 * block : 3 * block, :]),
            (doc_ref, a_refs[m].at[3 * block :, :]),
            (g_ref.at[:, cols], g_refs[m]),
        ]
        for source, target in parts:
            copies.append(pltpu.make_async_copy(source, target, sems.at[len(copies)]))
    for copy in copies:
        copy.start()
    for copy in copies:
        copy.wait()


def unpack_kernel(block, rank_ref, *refs):
    n = 8
    d_refs, outs, sems = refs[:n], refs[n : n + 3], refs[n + 3]
    copies = []
    for m in range(n):
        cols = pl.ds(pl.multiple_of((rank_ref[0] ^ m) * HEAD_DIM, HEAD_DIM), HEAD_DIM)
        for part, out in enumerate(outs):
            rows = slice(part * block, (part + 1) * block)
            copies.append(
                pltpu.make_async_copy(d_refs[m].at[rows, :], out.at[:, cols], sems.at[len(copies)])
            )
    for copy in copies:
        copy.start()
    for copy in copies:
        copy.wait()


def normed_kernel(block, rank_ref, stats_ref, *refs):
    n = 8
    o_refs, out_ref = refs[:n], refs[n]
    inv_rms = lax.rsqrt(stats_ref[0, 0:1, :] / (HEADS * HEAD_DIM) + norm_eps)
    spread = jnp.broadcast_to(inv_rms, (HEAD_DIM, block)).T
    for m in range(n):
        cols = pl.ds(pl.multiple_of((rank_ref[0] ^ m) * HEAD_DIM, HEAD_DIM), HEAD_DIM)
        out_ref[:, cols] = (o_refs[m][...].astype(F32) * spread).astype(BF16)


SMEM_SPEC = pl.BlockSpec(memory_space=pltpu.SMEM)
ANY_SPEC = pl.BlockSpec(memory_space=pl.ANY)
VMEM_SPEC = pl.BlockSpec(memory_space=pltpu.VMEM)


def shape_of(shape, dtype):
    return jax.ShapeDtypeStruct(shape, dtype)


def swap(value, m):
    if m == 0:
        return value
    n = lax.axis_size("seq")
    return lax.ppermute(value, "seq", [(s, s ^ m) for s in range(n)])


def sum_everywhere(stats):
    stats = stats + swap(stats, 1)
    stats = stats + swap(stats, 2) + swap(stats, 4) + swap(stats, 6)
    heads = lax.axis_size("head")
    parts = [
        lax.ppermute(stats, "head", [(s, (s + d) % heads) for s in range(heads)])
        for d in range(1, heads)
    ]
    return functools.reduce(jnp.add, parts, stats)


def by_head(queries, keys, values, grad_normed, docs):
    block, width_dev = queries.shape
    n = width_dev // HEAD_DIM
    rank = lax.axis_index("seq").reshape(1).astype(jnp.int32)
    doc_rows = jnp.pad(
        docs.astype(BF16).reshape(block // 128, 128), ((0, 16 - block // 128), (0, 0)),
        constant_values=4.0,
    )
    rows = 3 * block + 16
    params = pltpu.CompilerParams(vmem_limit_bytes=VMEM_BYTES)
    packed = pl.pallas_call(
        functools.partial(pack_kernel, block),
        out_shape=[shape_of((rows, HEAD_DIM), BF16)] * n + [shape_of((block, HEAD_DIM), BF16)] * n,
        in_specs=[SMEM_SPEC] + [ANY_SPEC] * 5,
        out_specs=[VMEM_SPEC] * (2 * n),
        scratch_shapes=[pltpu.SemaphoreType.DMA((5 * n,))],
        compiler_params=params,
        name="pack",
    )(rank, queries, keys, values, grad_normed, doc_rows)
    a = [swap(packed[m], m) for m in range(n)]
    g = [swap(packed[n + m], m) for m in range(n)]

    step = lambda *shape: pl.BlockSpec((1,) + shape, lambda i: (i,) + (0,) * len(shape))
    probs, out_t, out, inv_total, square = pl.pallas_call(
        functools.partial(forward_kernel, block),
        grid=(n,),
        out_shape=[
            shape_of((n, len(OFFSETS), block, block), BF16),
            shape_of((n, HEAD_DIM, block), F32),
            shape_of((n, block, HEAD_DIM), BF16),
            shape_of((n, 1, block), F32),
            shape_of((n, 1, block), F32),
        ],
        in_specs=[SMEM_SPEC] + [ANY_SPEC] * n,
        out_specs=[
            step(len(OFFSETS), block, block),
            step(HEAD_DIM, block),
            step(block, HEAD_DIM),
            step(1, block),
            step(1, block),
        ],
        scratch_shapes=[
            pltpu.VMEM((n, rows, HEAD_DIM), BF16),
            pltpu.VMEM((n, HEAD_DIM, block), BF16),
            pltpu.VMEM((len(OFFSETS), block, block), F32),
            pltpu.VMEM((1, block), F32),
            pltpu.VMEM((1, block), F32),
            pltpu.VMEM((HEAD_DIM, block), F32),
            pltpu.SMEM((3,), jnp.int32),
            pltpu.SemaphoreType.DMA((n,)),
        ],
        compiler_params=params,
        name="forward",
    )(rank, *a)

    stats = pl.pallas_call(
        functools.partial(project_kernel, block),
        out_shape=shape_of((2, n * block), F32),
        in_specs=[SMEM_SPEC] + [ANY_SPEC] * n + [VMEM_SPEC] * 2,
        out_specs=VMEM_SPEC,
        scratch_shapes=[
            pltpu.VMEM((n, block, HEAD_DIM), BF16),
            pltpu.SemaphoreType.DMA((n,)),
        ],
        compiler_params=params,
        name="project",
    )(rank, *g, out_t, square)
    stats = sum_everywhere(stats)

    home = [
        swap(lax.dynamic_index_in_dim(out, rank[0] ^ m, 0, keepdims=False), m) for m in range(n)
    ]
    stats_by_block = stats.reshape(2, n, block).transpose(1, 0, 2)
    own_stats = lax.dynamic_slice_in_dim(stats_by_block, rank[0], 1, axis=0)
    normed = pl.pallas_call(
        functools.partial(normed_kernel, block),
        out_shape=shape_of((block, width_dev), BF16),
        in_specs=[SMEM_SPEC] + [VMEM_SPEC] * (n + 1),
        out_specs=VMEM_SPEC,
        compiler_params=params,
        name="normed",
    )(rank, own_stats, *home)

    grads = pl.pallas_call(
        functools.partial(backward_kernel, block),
        grid=(n,),
        out_shape=[shape_of((3 * block, HEAD_DIM), BF16)] * n,
        in_specs=[SMEM_SPEC] + [ANY_SPEC] * (2 * n) + [
            step(len(OFFSETS), block, block),
            step(HEAD_DIM, block),
            step(1, block),
            step(2, block),
        ],
        out_specs=[pl.BlockSpec((3 * block, HEAD_DIM), lambda i: (0, 0))] * n,
        scratch_shapes=[
            pltpu.VMEM((n, rows, HEAD_DIM), BF16),
            pltpu.VMEM((n, block, HEAD_DIM), BF16),
            pltpu.VMEM((n, HEAD_DIM, block), BF16),
            pltpu.VMEM((n, block, HEAD_DIM), BF16),
            pltpu.VMEM((n, block, HEAD_DIM), F32),
            pltpu.VMEM((n, block, HEAD_DIM), F32),
            pltpu.VMEM((HEAD_DIM, block), F32),
            pltpu.SMEM((3,), jnp.int32),
            pltpu.SemaphoreType.DMA((n,)),
            pltpu.SemaphoreType.DMA((n,)),
        ],
        compiler_params=params,
        name="backward",
    )(rank, *a, *g, probs, out_t, inv_total, stats_by_block)
    back = [swap(grads[m], m) for m in range(n)]
    grad_outs = pl.pallas_call(
        functools.partial(unpack_kernel, block),
        out_shape=[shape_of((block, width_dev), BF16)] * 3,
        in_specs=[SMEM_SPEC] + [ANY_SPEC] * n,
        out_specs=[VMEM_SPEC] * 3,
        scratch_shapes=[pltpu.SemaphoreType.DMA((3 * n,))],
        compiler_params=params,
        name="unpack",
    )(rank, *back)
    return (normed, *grad_outs)


def from_behind(value, axis, steps):
    count = lax.axis_size(axis)
    initial, last = (max(0, -steps), min(count, count - steps))
    return lax.ppermute(value, axis, [(source, source + steps) for source in range(initial, last)])


def allowed_pairs(all_docs, own_docs, query_pos, seq_rank, offset, block_len):
    key_start = (seq_rank - offset) * block_len
    key_pos = key_start + jnp.arange(block_len, dtype=jnp.int32)
    key_docs = lax.dynamic_slice_in_dim(all_docs, jnp.maximum(key_start, 0), block_len)
    return (
        (key_pos[None, :] >= 0)
        & (key_pos[None, :] <= query_pos[:, None])
        & (key_docs[None, :] == own_docs[:, None])
    )


def masked_scores(query_heads, source, allowed, score_scale):
    key_heads = source[0].reshape(query_heads.shape)
    scores = (
        jnp.einsum("qhd,khd->hqk", query_heads, key_heads, preferred_element_type=jnp.float32)
        * score_scale
    )
    return jnp.where(allowed[None], scores, -jnp.inf)


def by_block(queries, keys, values, grad_normed, docs):
    block_len, width_dev = queries.shape
    heads_dev = width_dev // HEAD_DIM
    width = HEADS * HEAD_DIM
    score_scale = 1.0 / math.sqrt(HEAD_DIM)
    seq_rank = lax.axis_index("seq")
    levels = lax.axis_size("seq").bit_length() - 1
    distances = [2**exponent for exponent in range(levels)]
    all_docs = lax.all_gather(docs, "seq", axis=0, tiled=True)
    query_pos = seq_rank * block_len + jnp.arange(block_len, dtype=jnp.int32)
    query_heads = queries.reshape(block_len, heads_dev, HEAD_DIM)
    key_value = jnp.stack([keys, values])
    fetched = [from_behind(key_value, "seq", offset) for offset in distances]
    offsets = [0] + distances
    sources = [key_value] + fetched
    masks = [
        allowed_pairs(all_docs, docs, query_pos, seq_rank, offset, block_len) for offset in offsets
    ]
    shape_heads = (block_len, heads_dev, HEAD_DIM)
    row_max = jnp.full((heads_dev, block_len), -jnp.inf, jnp.float32)
    row_sum = jnp.zeros((heads_dev, block_len), jnp.float32)
    for source, allowed in zip(sources, masks):

        def update_stats(state, source_kv, allowed_now):
            old_max, old_sum = state
            scores = masked_scores(query_heads, source_kv, allowed_now, score_scale)
            new_max = jnp.maximum(old_max, jnp.max(scores, axis=-1))
            new_sum = old_sum * jnp.exp(old_max - new_max) + jnp.sum(
                jnp.exp(scores - new_max[..., None]), axis=-1
            )
            return (new_max, new_sum)

        def keep_stats(state, source_kv, allowed_now):
            return state

        row_max, row_sum = lax.cond(
            jnp.any(allowed), update_stats, keep_stats, (row_max, row_sum), source, allowed
        )
    log_total = row_max + jnp.log(row_sum)
    attn = jnp.zeros(shape_heads, jnp.float32)
    for source, allowed in zip(sources, masks):

        def forward_term(source_kv, allowed_now):
            scores = masked_scores(query_heads, source_kv, allowed_now, score_scale)
            prob_round = jnp.exp(scores - log_total[..., None]).astype(jnp.bfloat16)
            value_heads = source_kv[1].reshape(shape_heads)
            return jnp.einsum(
                "hqk,khd->qhd", prob_round, value_heads, preferred_element_type=jnp.float32
            )

        def empty_term(source_kv, allowed_now):
            return jnp.zeros(shape_heads, jnp.float32)

        attn = attn + lax.cond(jnp.any(allowed), forward_term, empty_term, source, allowed)
    attn_flat = attn.reshape(block_len, width_dev)
    cotangent = grad_normed.astype(jnp.float32)
    square_local = jnp.sum(attn_flat * attn_flat, axis=-1)
    square_total = lax.psum(square_local, "head")
    inv_rms = lax.rsqrt(square_total / width + norm_eps)
    normed = (attn_flat * inv_rms[:, None]).astype(jnp.bfloat16)
    projection = lax.psum(jnp.sum(cotangent * attn_flat, axis=-1), "head")
    dattn = (
        inv_rms[:, None] * cotangent - attn_flat * (inv_rms**3 * projection / width)[:, None]
    ).astype(jnp.bfloat16)
    dattn_heads = dattn.reshape(shape_heads)
    row_delta = jnp.sum(dattn_heads.astype(jnp.float32) * attn, axis=-1).T
    grad_query = jnp.zeros(shape_heads, jnp.float32)
    partials = []
    for source, allowed in zip(sources, masks):

        def backward_term(source_kv, allowed_now):
            scores = masked_scores(query_heads, source_kv, allowed_now, score_scale)
            prob_exact = jnp.exp(scores - log_total[..., None])
            prob_round = prob_exact.astype(jnp.bfloat16)
            key_heads = source_kv[0].reshape(shape_heads)
            value_heads = source_kv[1].reshape(shape_heads)
            dprob = jnp.einsum(
                "qhd,khd->hqk", dattn_heads, value_heads, preferred_element_type=jnp.float32
            )
            dscore = (prob_exact * (dprob - row_delta[..., None]) * score_scale).astype(
                jnp.bfloat16
            )
            query_term = jnp.einsum(
                "hqk,khd->qhd", dscore, key_heads, preferred_element_type=jnp.float32
            )
            key_term = jnp.einsum(
                "hqk,qhd->khd", dscore, query_heads, preferred_element_type=jnp.float32
            )
            value_term = jnp.einsum(
                "hqk,qhd->khd", prob_round, dattn_heads, preferred_element_type=jnp.float32
            )
            return (
                query_term,
                jnp.stack(
                    [
                        key_term.reshape(block_len, width_dev),
                        value_term.reshape(block_len, width_dev),
                    ]
                ),
            )

        def empty_pair(source_kv, allowed_now):
            return (
                jnp.zeros(shape_heads, jnp.float32),
                jnp.zeros((2, block_len, width_dev), jnp.float32),
            )

        query_term, pair_term = lax.cond(
            jnp.any(allowed), backward_term, empty_pair, source, allowed
        )
        grad_query = grad_query + query_term
        partials.append(pair_term)
    local_term = partials[0]
    far_terms = partials[1:]
    summed = local_term
    for offset, addend in zip(distances, far_terms):
        summed = summed + from_behind(addend.astype(jnp.bfloat16), "seq", -offset).astype(
            addend.dtype
        )
    grad_queries = grad_query.reshape(block_len, width_dev).astype(jnp.bfloat16)
    return (normed, grad_queries, summed[0].astype(jnp.bfloat16), summed[1].astype(jnp.bfloat16))


def body(queries, *others):
    block_len, width_dev = queries.shape
    if lax.axis_size("seq") == 8 and width_dev == 8 * HEAD_DIM and block_len == 512:
        return by_head(queries, *others)
    return by_block(queries, *others)


def solution(mesh):
    placed = (P("seq", "head"), P("seq", "head"), P("seq", "head"), P("seq", "head"), P("seq"))
    return jax.shard_map(
        body,
        mesh=mesh,
        in_specs=placed,
        out_specs=(P("seq", "head"), P("seq", "head"), P("seq", "head"), P("seq", "head")),
        check_vma=False,
    )
```

```python
import functools
import math

import jax
import jax.numpy as jnp
from jax import lax
from jax.experimental import pallas as pl
from jax.experimental.pallas import tpu as pltpu
from jax.sharding import PartitionSpec as P

HEADS = 32
HEAD_DIM = 128


norm_eps = 1e-06

OFFSETS = (0, 1, 2, 4)
NEG = -1e30
F32 = jnp.float32
BF16 = jnp.bfloat16
VMEM_BYTES = 60 * 1024 * 1024


ORDER = (0, 1, 2, 4, 6, 3, 5, 7)
FIRST_USE = [max(t + off for off in OFFSETS if t + off < 8) for t in range(8)]


def find_bounds(ids, bounds):
    ids = ids[...].astype(F32)
    for d in range(3):
        count = jnp.sum(jnp.where(ids < d + 0.5, 1.0, 0.0))
        bounds[d] = count.astype(jnp.int32)


def doc_of(position, bounds):
    doc = jnp.int32(0)
    for d in range(3):
        doc = doc + (position >= bounds[d]).astype(jnp.int32)
    return doc


def reach(i, block, bounds):
    first, last = doc_of(i * block, bounds), doc_of(i * block + block - 1, bounds)

    def active(off):
        return (i >= off) & (first == doc_of((i - off + 1) * block - 1, bounds))

    def full(off):
        return doc_of((i - off) * block, bounds) == last

    near = 1 + active(1).astype(jnp.int32) + active(2).astype(jnp.int32)
    return near, active(4), full(2), full(4)


def pieces(i, near, far, block):
    found = []
    if far:
        found.append((0, (i - 4) * block, block, False))
    if near > 1:
        found.append(((4 - near) * block, (i - near + 1) * block, (near - 1) * block, False))
    found.append((3 * block, i * block, block, True))
    return [(row, pl.multiple_of(key, block), size, own) for row, key, size, own in found]


def slots_of(near, far):
    return ([0] if far else []) + list(range(4 - near, 4))


def for_each_reach(i, block, bounds, body, split_full):
    near, far, full2, full4 = reach(i, block, bounds)
    pl.when(near == 1)(functools.partial(body, 1, False, True))
    pl.when(near == 2)(functools.partial(body, 2, False, True))
    alone = (near == 3) & jnp.logical_not(far)
    if not split_full:
        pl.when(alone)(functools.partial(body, 3, False, True))
        pl.when(far)(functools.partial(body, 3, True, True))
        return
    pl.when(alone & full2)(functools.partial(body, 3, False, False))
    pl.when(alone & jnp.logical_not(full2))(functools.partial(body, 3, False, True))
    pl.when(far & full4)(functools.partial(body, 3, True, False))
    pl.when(far & jnp.logical_not(full4))(functools.partial(body, 3, True, True))


def each_slot(i, block, bounds, act):
    near, far, _, _ = reach(i, block, bounds)
    act(3)
    pl.when(near > 1)(lambda: act(2))
    pl.when(near > 2)(lambda: act(1))
    pl.when(far)(lambda: act(0))


def doc_starts(i, block, bounds):
    pos = i * block + lax.broadcasted_iota(jnp.int32, (1, block), 1)
    start = jnp.zeros((1, block), jnp.int32)
    for d in range(3):
        start = jnp.where(pos >= bounds[d], jnp.maximum(start, bounds[d]), start)
    return pos, start


def nt_dot(a, b):
    return lax.dot_general(a, b, (((1,), (1,)), ((), ())), preferred_element_type=F32)


def nn_dot(a, b):
    return lax.dot_general(a, b, (((1,), (0,)), ((), ())), preferred_element_type=F32)


def parts_in(ref, t, block, held, sems):
    return [
        pltpu.make_async_copy(
            ref.at[part * block : (part + 1) * block, :],
            held.at[part, pl.ds(pl.multiple_of(t * block, block), block), :],
            sems.at[part, t],
        )
        for part in range(3)
    ]


def forward_kernel(block, rank_ref, *refs):
    n = 8
    a_refs = refs[:n]
    prob_ref, out_t_ref, out_ref, inv_ref, square_ref, bounds = refs[n : n + 6]
    held, ids, val_t, prob, out_t_keep, out_keep = refs[n + 6 : n + 12]
    total, acc, sems, id_sems, prob_sems, out_sems = refs[n + 12 :]
    rank = rank_ref[0]

    def ids_in(m, ref):
        return pltpu.make_async_copy(ref.at[3 * block :, :], ids.at[rank ^ m], id_sems.at[m])

    for m, ref in zip(ORDER, a_refs):
        ids_in(m, ref).start()
    for m, ref in zip(ORDER, a_refs):
        for copy in parts_in(ref, rank ^ m, block, held, sems):
            copy.start()
    for m, ref in zip(ORDER, a_refs):
        ids_in(m, ref).wait()
    find_bounds(ids, bounds)

    gain = math.log2(math.e) / math.sqrt(HEAD_DIM)

    def prob_out(i, slot):
        rows = slice(slot * block, (slot + 1) * block)
        return pltpu.make_async_copy(
            prob.at[i, rows, :], prob_ref.at[i, rows, :], prob_sems.at[i, slot]
        )

    def rows_out(i):
        return (
            pltpu.make_async_copy(out_t_keep.at[i], out_t_ref.at[i], out_sems.at[0, i]),
            pltpu.make_async_copy(out_keep.at[i], out_ref.at[i], out_sems.at[1, i]),
        )

    def one_block(i, carry):
        own_rows = pl.ds(pl.multiple_of(i * block, block), block)
        for copy in parts_in(a_refs[0], i, block, held, sems):
            copy.wait()
        val_t[:, own_rows] = held[2, own_rows, :].T
        query = held[0, own_rows, :]
        q_pos, q_start = doc_starts(i, block, bounds)

        def body(near, far, masked):
            found = pieces(i, near, far, block)
            scores, top = [], None
            for row, key, size, own in found:
                s = nt_dot(held[1, pl.ds(key, size), :], query) * gain
                if masked or own:
                    k_pos = key + lax.broadcasted_iota(jnp.int32, (size, 1), 0)
                    if not masked:
                        keep = k_pos <= q_pos
                    elif own:
                        keep = (k_pos >= q_start) & (k_pos <= q_pos)
                    else:
                        keep = k_pos >= q_start
                    s = jnp.where(keep, s, NEG)
                scores.append(s)
                peak = jnp.max(s, axis=0, keepdims=True)
                top = peak if top is None else jnp.maximum(top, peak)
            for number, ((row, key, size, own), s) in enumerate(zip(found, scores)):
                p = jnp.exp2(s - top)
                line = jnp.sum(p, axis=0, keepdims=True)
                pb = p.astype(BF16)
                prob[i, row : row + size, :] = pb
                term = nn_dot(val_t[:, pl.ds(key, size)], pb)
                total[...] = line if number == 0 else total[...] + line
                acc[...] = term if number == 0 else acc[...] + term
            for slot in slots_of(near, far):
                prob_out(i, slot).start()

        for_each_reach(i, block, bounds, body, True)

        inv = 1.0 / total[...]
        out_t = acc[...] * inv
        out_t_keep[i] = out_t
        out_keep[i] = out_t.T.astype(BF16)
        inv_ref[i] = inv
        square_ref[i] = jnp.sum(out_t * out_t, axis=0, keepdims=True)
        for copy in rows_out(i):
            copy.start()
        return carry

    lax.fori_loop(0, n, one_block, 0)

    def finish(i, carry):
        each_slot(i, block, bounds, lambda slot: prob_out(i, slot).wait())
        for copy in rows_out(i):
            copy.wait()
        return carry

    lax.fori_loop(0, n, finish, 0)


def project_kernel(block, rank_ref, *refs):
    n = 8
    g_refs = refs[:n]
    out_ref, square_ref, stats_ref, held, sems = refs[n:]
    rank = rank_ref[0]
    copies = [
        pltpu.make_async_copy(ref, held.at[rank ^ m], sems.at[m]) for m, ref in zip(ORDER, g_refs)
    ]
    for copy in copies:
        copy.start()
    for copy in copies:
        copy.wait()
    ones = jnp.ones((16, HEAD_DIM), BF16)
    for t in range(n):
        x = held[t].astype(F32) * out_ref[t].astype(F32)
        high = x.astype(BF16)
        low = (x - high.astype(F32)).astype(BF16)
        cols = slice(t * block, (t + 1) * block)
        stats_ref[0:1, cols] = square_ref[t]
        stats_ref[1:2, cols] = (nt_dot(ones, high) + nt_dot(ones, low))[0:1]


def backward_kernel(block, rank_ref, bounds, *refs):
    n = 8
    a_refs, g_refs = refs[:n], refs[n : 2 * n]
    prob_ref, out_t_ref, inv_ref, stats_ref = refs[2 * n : 2 * n + 4]
    d_refs = refs[2 * n + 4 : 3 * n + 4]
    held, cot, key_t, prob, out_t_keep, stage, grad_k, grad_v, acc = refs[3 * n + 4 : 3 * n + 13]
    sems, g_sems, prob_sems, out_sems, d_sems = refs[3 * n + 13 :]
    rank = rank_ref[0]
    scale = 1.0 / math.sqrt(HEAD_DIM)
    width = HEADS * HEAD_DIM

    def cot_in(ref, t):
        return pltpu.make_async_copy(ref, cot.at[t], g_sems.at[t])

    def out_in(i):
        return pltpu.make_async_copy(out_t_ref.at[i], out_t_keep.at[i], out_sems.at[i])

    def prob_in(i, slot):
        rows = slice(slot * block, (slot + 1) * block)
        return pltpu.make_async_copy(
            prob_ref.at[i, rows, :], prob.at[i, rows, :], prob_sems.at[i, slot]
        )

    for m, ref in zip(ORDER, g_refs):
        cot_in(ref, rank ^ m).start()
    for m, ref in zip(ORDER, a_refs):
        for copy in parts_in(ref, rank ^ m, block, held, sems):
            copy.start()

    def fetch(step, carry):
        i = n - 1 - step
        out_in(i).start()
        each_slot(i, block, bounds, lambda slot: prob_in(i, slot).start())
        return carry

    lax.fori_loop(0, n, fetch, 0)
    grad_k[...] = jnp.zeros_like(grad_k)
    grad_v[...] = jnp.zeros_like(grad_v)

    def one_block(step, carry):
        i = n - 1 - step
        cot_in(g_refs[0], i).wait()
        out_in(i).wait()
        inv_rms = lax.rsqrt(stats_ref[i, 0:1, :] / width + norm_eps)
        coef = inv_rms * inv_rms * inv_rms * stats_ref[i, 1:2, :] / width
        out_t = out_t_keep[i]
        dattn_t = (inv_rms * cot[i].astype(F32).T - out_t * coef) * inv_ref[i]
        dattn_tb = dattn_t.astype(BF16)
        dattn_f = dattn_tb.astype(F32)
        delta = jnp.sum(dattn_f * out_t, axis=0, keepdims=True)
        dattn = dattn_f.T.astype(BF16)
        for first in sorted(set(FIRST_USE)):

            @pl.when(i == first)
            def _():
                for t in range(n):
                    if FIRST_USE[t] == first:
                        for copy in parts_in(a_refs[0], t, block, held, sems):
                            copy.wait()
                        cols = slice(t * block, (t + 1) * block)
                        key_t[:, cols] = held[1, cols, :].T

        own_rows = pl.ds(pl.multiple_of(i * block, block), block)
        query = held[0, own_rows, :]

        def body(near, far, masked):
            for slot in slots_of(near, far):
                prob_in(i, slot).wait()
            for number, (row, key, size, own) in enumerate(pieces(i, near, far, block)):
                rows = pl.ds(key, size)
                pb = prob[i, row : row + size, :]
                dprob = nn_dot(held[2, rows, :], dattn_tb)
                ds = (pb.astype(F32) * (dprob - delta)).astype(BF16)
                term = nn_dot(key_t[:, rows], ds)
                acc[...] = term if number == 0 else acc[...] + term
                grad_k[rows, :] += nn_dot(ds, query)
                grad_v[rows, :] += nn_dot(pb, dattn)

        for_each_reach(i, block, bounds, body, False)

        stage[i, 0:block, :] = (acc[...] * scale).T.astype(BF16)
        stage[i, block : 2 * block, :] = (grad_k[own_rows, :] * scale).astype(BF16)
        stage[i, 2 * block :, :] = grad_v[own_rows, :].astype(BF16)
        for m, ref in zip(ORDER, d_refs):

            @pl.when((rank ^ m) == i)
            def _():
                pltpu.make_async_copy(stage.at[i], ref, d_sems.at[m]).start()

        return carry

    lax.fori_loop(0, n, one_block, 0)
    for m, ref in zip(ORDER, d_refs):
        pltpu.make_async_copy(stage.at[0], ref, d_sems.at[m]).wait()


def pack_kernel(block, rank_ref, q_ref, k_ref, v_ref, g_ref, doc_ref, *refs):
    n = 8
    a_refs, g_refs, sems = refs[:n], refs[n : 2 * n], refs[2 * n]
    copies = []
    for index, m in enumerate(ORDER):
        cols = pl.ds(pl.multiple_of((rank_ref[0] ^ m) * HEAD_DIM, HEAD_DIM), HEAD_DIM)
        parts = [
            (q_ref.at[:, cols], a_refs[index].at[0:block, :]),
            (k_ref.at[:, cols], a_refs[index].at[block : 2 * block, :]),
            (v_ref.at[:, cols], a_refs[index].at[2 * block : 3 * block, :]),
            (g_ref.at[:, cols], g_refs[index]),
        ]
        for source, target in parts:
            copies.append(pltpu.make_async_copy(source, target, sems.at[len(copies)]))
    for copy in copies:
        copy.start()
    row = lax.broadcasted_iota(jnp.int32, (16, HEAD_DIM), 0)
    ids = jnp.full((16, HEAD_DIM), 4.0, F32)
    for k in range(block // HEAD_DIM):
        part = doc_ref[0:1, k * HEAD_DIM : (k + 1) * HEAD_DIM].astype(F32)
        ids = jnp.where(row == k, part, ids)
    for ref in a_refs:
        ref[3 * block :, :] = ids.astype(BF16)
    for copy in copies:
        copy.wait()


def unpack_kernel(block, rank_ref, *refs):
    n = 8
    d_refs, outs, sems = refs[:n], refs[n : n + 3], refs[n + 3]
    copies = []
    for m, ref in zip(ORDER, d_refs):
        cols = pl.ds(pl.multiple_of((rank_ref[0] ^ m) * HEAD_DIM, HEAD_DIM), HEAD_DIM)
        for part, out in enumerate(outs):
            rows = slice(part * block, (part + 1) * block)
            copies.append(
                pltpu.make_async_copy(ref.at[rows, :], out.at[:, cols], sems.at[len(copies)])
            )
    for copy in copies:
        copy.start()
    for copy in copies:
        copy.wait()


def normed_kernel(block, rank_ref, stats_ref, *refs):
    n = 8
    o_refs, out_ref = refs[:n], refs[n]
    inv_rms = lax.rsqrt(stats_ref[0, 0:1, :] / (HEADS * HEAD_DIM) + norm_eps)
    spread = jnp.broadcast_to(inv_rms, (HEAD_DIM, block)).T
    for m, ref in zip(ORDER, o_refs):
        cols = pl.ds(pl.multiple_of((rank_ref[0] ^ m) * HEAD_DIM, HEAD_DIM), HEAD_DIM)
        out_ref[:, cols] = (ref[...].astype(F32) * spread).astype(BF16)


SMEM_SPEC = pl.BlockSpec(memory_space=pltpu.SMEM)
ANY_SPEC = pl.BlockSpec(memory_space=pl.ANY)
VMEM_SPEC = pl.BlockSpec(memory_space=pltpu.VMEM)


def shape_of(shape, dtype):
    return jax.ShapeDtypeStruct(shape, dtype)


def swap(value, m):
    if m == 0:
        return value
    n = lax.axis_size("seq")
    return lax.ppermute(value, "seq", [(s, s ^ m) for s in range(n)])


def swap_all(parts):
    return [swap(part, m) for m, part in zip(ORDER, parts)]


def sum_everywhere(stats):
    stats = stats + swap(stats, 1)
    stats = stats + swap(stats, 2) + swap(stats, 4) + swap(stats, 6)
    heads = lax.axis_size("head")
    parts = [
        lax.ppermute(stats, "head", [(s, (s + d) % heads) for s in range(heads)])
        for d in range(1, heads)
    ]
    return functools.reduce(jnp.add, parts, stats)


def run_forward(rank, a, block):
    n = len(a)
    return pl.pallas_call(
        functools.partial(forward_kernel, block),
        out_shape=[
            shape_of((n, 4 * block, block), BF16),
            shape_of((n, HEAD_DIM, block), F32),
            shape_of((n, block, HEAD_DIM), BF16),
            shape_of((n, 1, block), F32),
            shape_of((n, 1, block), F32),
            shape_of((3,), jnp.int32),
        ],
        in_specs=[SMEM_SPEC] + [ANY_SPEC] * n,
        out_specs=[ANY_SPEC] * 3 + [VMEM_SPEC] * 2 + [SMEM_SPEC],
        scratch_shapes=[
            pltpu.VMEM((3, n * block, HEAD_DIM), BF16),
            pltpu.VMEM((n, 16, HEAD_DIM), BF16),
            pltpu.VMEM((HEAD_DIM, n * block), BF16),
            pltpu.VMEM((n, 4 * block, block), BF16),
            pltpu.VMEM((n, HEAD_DIM, block), F32),
            pltpu.VMEM((n, block, HEAD_DIM), BF16),
            pltpu.VMEM((1, block), F32),
            pltpu.VMEM((HEAD_DIM, block), F32),
            pltpu.SemaphoreType.DMA((3, n)),
            pltpu.SemaphoreType.DMA((n,)),
            pltpu.SemaphoreType.DMA((n, len(OFFSETS))),
            pltpu.SemaphoreType.DMA((2, n)),
        ],
        compiler_params=pltpu.CompilerParams(vmem_limit_bytes=VMEM_BYTES),
        name="forward",
    )(rank, *a)


def run_project(rank, g, out, square, block):
    n = len(g)
    return pl.pallas_call(
        functools.partial(project_kernel, block),
        out_shape=shape_of((2, n * block), F32),
        in_specs=[SMEM_SPEC] + [ANY_SPEC] * n + [VMEM_SPEC] * 2,
        out_specs=VMEM_SPEC,
        scratch_shapes=[
            pltpu.VMEM((n, block, HEAD_DIM), BF16),
            pltpu.SemaphoreType.DMA((n,)),
        ],
        compiler_params=pltpu.CompilerParams(vmem_limit_bytes=VMEM_BYTES),
        name="project",
    )(rank, *g, out, square)


def run_backward(rank, bounds, a, g, probs, out_t, inv_total, stats_by_block, block):
    n = len(a)
    return pl.pallas_call(
        functools.partial(backward_kernel, block),
        out_shape=[shape_of((3 * block, HEAD_DIM), BF16)] * n,
        in_specs=[SMEM_SPEC] * 2 + [ANY_SPEC] * (2 * n + 2) + [VMEM_SPEC] * 2,
        out_specs=[ANY_SPEC] * n,
        scratch_shapes=[
            pltpu.VMEM((3, n * block, HEAD_DIM), BF16),
            pltpu.VMEM((n, block, HEAD_DIM), BF16),
            pltpu.VMEM((HEAD_DIM, n * block), BF16),
            pltpu.VMEM((n, 4 * block, block), BF16),
            pltpu.VMEM((n, HEAD_DIM, block), F32),
            pltpu.VMEM((n, 3 * block, HEAD_DIM), BF16),
            pltpu.VMEM((n * block, HEAD_DIM), F32),
            pltpu.VMEM((n * block, HEAD_DIM), F32),
            pltpu.VMEM((HEAD_DIM, block), F32),
            pltpu.SemaphoreType.DMA((3, n)),
            pltpu.SemaphoreType.DMA((n,)),
            pltpu.SemaphoreType.DMA((n, len(OFFSETS))),
            pltpu.SemaphoreType.DMA((n,)),
            pltpu.SemaphoreType.DMA((n,)),
        ],
        compiler_params=pltpu.CompilerParams(vmem_limit_bytes=VMEM_BYTES),
        name="backward",
    )(rank, bounds, *a, *g, probs, out_t, inv_total, stats_by_block)


def core_test(rank, a, g, stats):
    block, n = 512, 8
    a = [a[m] for m in ORDER]
    g = [g[m] for m in ORDER]
    probs, out_t, out, inv_total, square, bounds = run_forward(rank, a, block)
    s = run_project(rank, g, out, square, block)
    by = stats.reshape(2, n, block).transpose(1, 0, 2)
    grads = run_backward(rank, bounds, a, g, probs, out_t, inv_total, by, block)
    grads = [grads[ORDER.index(m)] for m in range(n)]
    return [out, s, *grads]


def by_head(queries, keys, values, grad_normed, docs):
    block, width_dev = queries.shape
    n = width_dev // HEAD_DIM
    rank = lax.axis_index("seq").reshape(1).astype(jnp.int32)
    rows = 3 * block + 16
    params = pltpu.CompilerParams(vmem_limit_bytes=VMEM_BYTES)
    packed = pl.pallas_call(
        functools.partial(pack_kernel, block),
        out_shape=[shape_of((rows, HEAD_DIM), BF16)] * n + [shape_of((block, HEAD_DIM), BF16)] * n,
        in_specs=[SMEM_SPEC] + [ANY_SPEC] * 4 + [VMEM_SPEC],
        out_specs=[VMEM_SPEC] * (2 * n),
        scratch_shapes=[pltpu.SemaphoreType.DMA((4 * n,))],
        compiler_params=params,
        name="pack",
    )(rank, queries, keys, values, grad_normed, docs.reshape(1, block))
    a = swap_all(packed[:n])
    first, packed_g = lax.optimization_barrier((a[2], list(packed[n:])))
    a[2] = first
    g = swap_all(packed_g)

    probs, out_t, out, inv_total, square, bounds = run_forward(rank, a, block)
    stats = run_project(rank, g, out, square, block)
    stats = sum_everywhere(stats)

    home = swap_all(
        [lax.dynamic_index_in_dim(out, rank[0] ^ m, 0, keepdims=False) for m in ORDER]
    )
    home, stats = lax.optimization_barrier((home, stats))
    stats_by_block = stats.reshape(2, n, block).transpose(1, 0, 2)
    own_stats = lax.dynamic_slice_in_dim(stats_by_block, rank[0], 1, axis=0)
    normed = pl.pallas_call(
        functools.partial(normed_kernel, block),
        out_shape=shape_of((block, width_dev), BF16),
        in_specs=[SMEM_SPEC] + [VMEM_SPEC] * (n + 1),
        out_specs=VMEM_SPEC,
        compiler_params=params,
        name="normed",
    )(rank, own_stats, *home)

    grads = run_backward(rank, bounds, a, g, probs, out_t, inv_total, stats_by_block, block)
    back = swap_all(grads)
    grad_outs = pl.pallas_call(
        functools.partial(unpack_kernel, block),
        out_shape=[shape_of((block, width_dev), BF16)] * 3,
        in_specs=[SMEM_SPEC] + [ANY_SPEC] * n,
        out_specs=[VMEM_SPEC] * 3,
        scratch_shapes=[pltpu.SemaphoreType.DMA((3 * n,))],
        compiler_params=params,
        name="unpack",
    )(rank, *back)
    return (normed, *grad_outs)


def from_behind(value, axis, steps):
    count = lax.axis_size(axis)
    initial, last = (max(0, -steps), min(count, count - steps))
    return lax.ppermute(value, axis, [(source, source + steps) for source in range(initial, last)])


def allowed_pairs(all_docs, own_docs, query_pos, seq_rank, offset, block_len):
    key_start = (seq_rank - offset) * block_len
    key_pos = key_start + jnp.arange(block_len, dtype=jnp.int32)
    key_docs = lax.dynamic_slice_in_dim(all_docs, jnp.maximum(key_start, 0), block_len)
    return (
        (key_pos[None, :] >= 0)
        & (key_pos[None, :] <= query_pos[:, None])
        & (key_docs[None, :] == own_docs[:, None])
    )


def masked_scores(query_heads, source, allowed, score_scale):
    key_heads = source[0].reshape(query_heads.shape)
    scores = (
        jnp.einsum("qhd,khd->hqk", query_heads, key_heads, preferred_element_type=jnp.float32)
        * score_scale
    )
    return jnp.where(allowed[None], scores, -jnp.inf)


def by_block(queries, keys, values, grad_normed, docs):
    block_len, width_dev = queries.shape
    heads_dev = width_dev // HEAD_DIM
    width = HEADS * HEAD_DIM
    score_scale = 1.0 / math.sqrt(HEAD_DIM)
    seq_rank = lax.axis_index("seq")
    levels = lax.axis_size("seq").bit_length() - 1
    distances = [2**exponent for exponent in range(levels)]
    all_docs = lax.all_gather(docs, "seq", axis=0, tiled=True)
    query_pos = seq_rank * block_len + jnp.arange(block_len, dtype=jnp.int32)
    query_heads = queries.reshape(block_len, heads_dev, HEAD_DIM)
    key_value = jnp.stack([keys, values])
    fetched = [from_behind(key_value, "seq", offset) for offset in distances]
    offsets = [0] + distances
    sources = [key_value] + fetched
    masks = [
        allowed_pairs(all_docs, docs, query_pos, seq_rank, offset, block_len) for offset in offsets
    ]
    shape_heads = (block_len, heads_dev, HEAD_DIM)
    row_max = jnp.full((heads_dev, block_len), -jnp.inf, jnp.float32)
    row_sum = jnp.zeros((heads_dev, block_len), jnp.float32)
    for source, allowed in zip(sources, masks):

        def update_stats(state, source_kv, allowed_now):
            old_max, old_sum = state
            scores = masked_scores(query_heads, source_kv, allowed_now, score_scale)
            new_max = jnp.maximum(old_max, jnp.max(scores, axis=-1))
            new_sum = old_sum * jnp.exp(old_max - new_max) + jnp.sum(
                jnp.exp(scores - new_max[..., None]), axis=-1
            )
            return (new_max, new_sum)

        def keep_stats(state, source_kv, allowed_now):
            return state

        row_max, row_sum = lax.cond(
            jnp.any(allowed), update_stats, keep_stats, (row_max, row_sum), source, allowed
        )
    log_total = row_max + jnp.log(row_sum)
    attn = jnp.zeros(shape_heads, jnp.float32)
    for source, allowed in zip(sources, masks):

        def forward_term(source_kv, allowed_now):
            scores = masked_scores(query_heads, source_kv, allowed_now, score_scale)
            prob_round = jnp.exp(scores - log_total[..., None]).astype(jnp.bfloat16)
            value_heads = source_kv[1].reshape(shape_heads)
            return jnp.einsum(
                "hqk,khd->qhd", prob_round, value_heads, preferred_element_type=jnp.float32
            )

        def empty_term(source_kv, allowed_now):
            return jnp.zeros(shape_heads, jnp.float32)

        attn = attn + lax.cond(jnp.any(allowed), forward_term, empty_term, source, allowed)
    attn_flat = attn.reshape(block_len, width_dev)
    cotangent = grad_normed.astype(jnp.float32)
    square_local = jnp.sum(attn_flat * attn_flat, axis=-1)
    square_total = lax.psum(square_local, "head")
    inv_rms = lax.rsqrt(square_total / width + norm_eps)
    normed = (attn_flat * inv_rms[:, None]).astype(jnp.bfloat16)
    projection = lax.psum(jnp.sum(cotangent * attn_flat, axis=-1), "head")
    dattn = (
        inv_rms[:, None] * cotangent - attn_flat * (inv_rms**3 * projection / width)[:, None]
    ).astype(jnp.bfloat16)
    dattn_heads = dattn.reshape(shape_heads)
    row_delta = jnp.sum(dattn_heads.astype(jnp.float32) * attn, axis=-1).T
    grad_query = jnp.zeros(shape_heads, jnp.float32)
    partials = []
    for source, allowed in zip(sources, masks):

        def backward_term(source_kv, allowed_now):
            scores = masked_scores(query_heads, source_kv, allowed_now, score_scale)
            prob_exact = jnp.exp(scores - log_total[..., None])
            prob_round = prob_exact.astype(jnp.bfloat16)
            key_heads = source_kv[0].reshape(shape_heads)
            value_heads = source_kv[1].reshape(shape_heads)
            dprob = jnp.einsum(
                "qhd,khd->hqk", dattn_heads, value_heads, preferred_element_type=jnp.float32
            )
            dscore = (prob_exact * (dprob - row_delta[..., None]) * score_scale).astype(
                jnp.bfloat16
            )
            query_term = jnp.einsum(
                "hqk,khd->qhd", dscore, key_heads, preferred_element_type=jnp.float32
            )
            key_term = jnp.einsum(
                "hqk,qhd->khd", dscore, query_heads, preferred_element_type=jnp.float32
            )
            value_term = jnp.einsum(
                "hqk,qhd->khd", prob_round, dattn_heads, preferred_element_type=jnp.float32
            )
            return (
                query_term,
                jnp.stack(
                    [
                        key_term.reshape(block_len, width_dev),
                        value_term.reshape(block_len, width_dev),
                    ]
                ),
            )

        def empty_pair(source_kv, allowed_now):
            return (
                jnp.zeros(shape_heads, jnp.float32),
                jnp.zeros((2, block_len, width_dev), jnp.float32),
            )

        query_term, pair_term = lax.cond(
            jnp.any(allowed), backward_term, empty_pair, source, allowed
        )
        grad_query = grad_query + query_term
        partials.append(pair_term)
    local_term = partials[0]
    far_terms = partials[1:]
    summed = local_term
    for offset, addend in zip(distances, far_terms):
        summed = summed + from_behind(addend.astype(jnp.bfloat16), "seq", -offset).astype(
            addend.dtype
        )
    grad_queries = grad_query.reshape(block_len, width_dev).astype(jnp.bfloat16)
    return (normed, grad_queries, summed[0].astype(jnp.bfloat16), summed[1].astype(jnp.bfloat16))


def body(queries, *others):
    block_len, width_dev = queries.shape
    if lax.axis_size("seq") == 8 and width_dev == 8 * HEAD_DIM and block_len == 512:
        return by_head(queries, *others)
    return by_block(queries, *others)


def solution(mesh):
    placed = (P("seq", "head"), P("seq", "head"), P("seq", "head"), P("seq", "head"), P("seq"))
    return jax.shard_map(
        body,
        mesh=mesh,
        in_specs=placed,
        out_specs=(P("seq", "head"), P("seq", "head"), P("seq", "head"), P("seq", "head")),
        check_vma=False,
    )
```

```python
import functools
import math

import jax
import jax.numpy as jnp
from jax import lax
from jax.experimental import pallas as pl
from jax.experimental.pallas import tpu as pltpu
from jax.sharding import PartitionSpec as P

HEADS = 32
HEAD_DIM = 128


norm_eps = 1e-06

OFFSETS = (0, 1, 2, 4)
NEG = -1e30
F32 = jnp.float32
BF16 = jnp.bfloat16
VMEM_BYTES = 60 * 1024 * 1024


ORDER = (0, 1, 2, 4, 6, 3, 5, 7)
TIE = 3
FIRST_USE = [max(t + off for off in OFFSETS if t + off < 8) for t in range(8)]


def find_bounds(ids, bounds):
    ids = ids[...].astype(F32)
    for d in range(3):
        count = jnp.sum(jnp.where(ids < d + 0.5, 1.0, 0.0))
        bounds[d] = count.astype(jnp.int32)


def doc_of(position, bounds):
    doc = jnp.int32(0)
    for d in range(3):
        doc = doc + (position >= bounds[d]).astype(jnp.int32)
    return doc


def reach(i, block, bounds):
    first, last = doc_of(i * block, bounds), doc_of(i * block + block - 1, bounds)

    def active(off):
        return (i >= off) & (first == doc_of((i - off + 1) * block - 1, bounds))

    def full(off):
        return doc_of((i - off) * block, bounds) == last

    near = 1 + active(1).astype(jnp.int32) + active(2).astype(jnp.int32)
    return near, active(4), full(2), full(4)


def pieces(i, near, far, block):
    found = []
    if far:
        found.append((0, (i - 4) * block, block, False))
    if near > 1:
        found.append(((4 - near) * block, (i - near + 1) * block, (near - 1) * block, False))
    found.append((3 * block, i * block, block, True))
    return [(row, pl.multiple_of(key, block), size, own) for row, key, size, own in found]


def slots_of(near, far):
    return ([0] if far else []) + list(range(4 - near, 4))


def for_each_reach(i, block, bounds, body, split_full):
    near, far, full2, full4 = reach(i, block, bounds)
    pl.when(near == 1)(functools.partial(body, 1, False, True))
    pl.when(near == 2)(functools.partial(body, 2, False, True))
    alone = (near == 3) & jnp.logical_not(far)
    if not split_full:
        pl.when(alone)(functools.partial(body, 3, False, True))
        pl.when(far)(functools.partial(body, 3, True, True))
        return
    pl.when(alone & full2)(functools.partial(body, 3, False, False))
    pl.when(alone & jnp.logical_not(full2))(functools.partial(body, 3, False, True))
    pl.when(far & full4)(functools.partial(body, 3, True, False))
    pl.when(far & jnp.logical_not(full4))(functools.partial(body, 3, True, True))


def each_slot(i, block, bounds, act):
    near, far, _, _ = reach(i, block, bounds)
    act(3)
    pl.when(near > 1)(lambda: act(2))
    pl.when(near > 2)(lambda: act(1))
    pl.when(far)(lambda: act(0))


def doc_starts(i, block, bounds):
    pos = i * block + lax.broadcasted_iota(jnp.int32, (1, block), 1)
    start = jnp.zeros((1, block), jnp.int32)
    for d in range(3):
        start = jnp.where(pos >= bounds[d], jnp.maximum(start, bounds[d]), start)
    return pos, start


def nt_dot(a, b):
    return lax.dot_general(a, b, (((1,), (1,)), ((), ())), preferred_element_type=F32)


def nn_dot(a, b):
    return lax.dot_general(a, b, (((1,), (0,)), ((), ())), preferred_element_type=F32)


def parts_in(ref, t, block, held, sems):
    return [
        pltpu.make_async_copy(
            ref.at[part * block : (part + 1) * block, :],
            held.at[part, pl.ds(pl.multiple_of(t * block, block), block), :],
            sems.at[part, t],
        )
        for part in range(2)
    ]


def score_kernel(block, rank_ref, *refs):
    n = 8
    a_refs = refs[:n]
    prob_ref, inv_ref, bounds = refs[n : n + 3]
    held, ids, prob, sems, id_sems, prob_sems = refs[n + 3 :]
    rank = rank_ref[0]

    def ids_in(m, ref):
        return pltpu.make_async_copy(ref.at[2 * block :, :], ids.at[rank ^ m], id_sems.at[m])

    for m, ref in zip(ORDER, a_refs):
        ids_in(m, ref).start()
    for m, ref in zip(ORDER, a_refs):
        for copy in parts_in(ref, rank ^ m, block, held, sems):
            copy.start()
    for m, ref in zip(ORDER, a_refs):
        ids_in(m, ref).wait()
    find_bounds(ids, bounds)

    gain = math.log2(math.e) / math.sqrt(HEAD_DIM)

    def prob_out(i, slot):
        rows = slice(slot * block, (slot + 1) * block)
        return pltpu.make_async_copy(
            prob.at[i, rows, :], prob_ref.at[i, rows, :], prob_sems.at[i, slot]
        )

    def one_block(i, carry):
        own_rows = pl.ds(pl.multiple_of(i * block, block), block)
        for copy in parts_in(a_refs[0], i, block, held, sems):
            copy.wait()
        query = held[0, own_rows, :]
        q_pos, q_start = doc_starts(i, block, bounds)

        def body(near, far, masked):
            found = pieces(i, near, far, block)
            scores, top = [], None
            for row, key, size, own in found:
                s = nt_dot(held[1, pl.ds(key, size), :], query) * gain
                if masked or own:
                    k_pos = key + lax.broadcasted_iota(jnp.int32, (size, 1), 0)
                    if not masked:
                        keep = k_pos <= q_pos
                    elif own:
                        keep = (k_pos >= q_start) & (k_pos <= q_pos)
                    else:
                        keep = k_pos >= q_start
                    s = jnp.where(keep, s, NEG)
                scores.append(s)
                peak = jnp.max(s, axis=0, keepdims=True)
                top = peak if top is None else jnp.maximum(top, peak)
            total = None
            for (row, key, size, own), s in zip(found, scores):
                p = jnp.exp2(s - top)
                line = jnp.sum(p, axis=0, keepdims=True)
                prob[i, row : row + size, :] = p.astype(BF16)
                total = line if total is None else total + line
            inv_ref[i] = 1.0 / total
            for slot in slots_of(near, far):
                prob_out(i, slot).start()

        for_each_reach(i, block, bounds, body, True)
        return carry

    lax.fori_loop(0, n, one_block, 0)

    def finish(i, carry):
        each_slot(i, block, bounds, lambda slot: prob_out(i, slot).wait())
        return carry

    lax.fori_loop(0, n, finish, 0)


def value_in(vg_ref, t, block, values, sems):
    return pltpu.make_async_copy(
        vg_ref.at[0:block, :],
        values.at[pl.ds(pl.multiple_of(t * block, block), block), :],
        sems.at[0, t],
    )


def cot_in(vg_ref, t, block, cot, sems):
    return pltpu.make_async_copy(vg_ref.at[block:, :], cot.at[t], sems.at[1, t])


def fetch_probs(n, block, bounds, prob_ref, prob, sems):
    def prob_in(i, slot):
        rows = slice(slot * block, (slot + 1) * block)
        return pltpu.make_async_copy(prob_ref.at[i, rows, :], prob.at[i, rows, :], sems.at[i, slot])

    return prob_in


def attend_kernel(block, rank_ref, bounds, *refs):
    n = 8
    vg_refs = refs[:n]
    prob_ref, inv_ref, out_t_ref, out_ref, stats_ref = refs[n : n + 5]
    values, cot, val_t, prob, out_t_keep, out_keep, acc, vg_sems, prob_sems, out_sems = refs[n + 5 :]
    vg_ref = vg_refs[0]
    prob_in = fetch_probs(n, block, bounds, prob_ref, prob, prob_sems)

    def rows_out(i):
        return (
            pltpu.make_async_copy(out_t_keep.at[i], out_t_ref.at[i], out_sems.at[0, i]),
            pltpu.make_async_copy(out_keep.at[i], out_ref.at[i], out_sems.at[1, i]),
        )

    for m, ref in zip(ORDER, vg_refs):
        value_in(ref, rank_ref[0] ^ m, block, values, vg_sems).start()
        cot_in(ref, rank_ref[0] ^ m, block, cot, vg_sems).start()
    for t in range(n):
        each_slot(t, block, bounds, lambda slot: prob_in(t, slot).start())
    ones = jnp.ones((16, HEAD_DIM), BF16)

    def one_block(i, carry):
        own_rows = pl.ds(pl.multiple_of(i * block, block), block)
        value_in(vg_ref, i, block, values, vg_sems).wait()
        val_t[:, own_rows] = values[own_rows, :].T

        def body(near, far, masked):
            for slot in slots_of(near, far):
                prob_in(i, slot).wait()
            out = None
            for row, key, size, own in pieces(i, near, far, block):
                term = nn_dot(val_t[:, pl.ds(key, size)], prob[i, row : row + size, :])
                out = term if out is None else out + term
            acc[...] = out

        for_each_reach(i, block, bounds, body, False)

        out_t = acc[...] * inv_ref[i]
        out_t_keep[i] = out_t
        out = out_t.T
        out_keep[i] = out.astype(BF16)
        for copy in rows_out(i):
            copy.start()
        stats_ref[0, i] = jnp.sum(out_t * out_t, axis=0, keepdims=True)
        cot_in(vg_ref, i, block, cot, vg_sems).wait()
        x = cot[i].astype(F32) * out
        high = x.astype(BF16)
        low = (x - high.astype(F32)).astype(BF16)
        stats_ref[1, i] = (nt_dot(ones, high) + nt_dot(ones, low))[0:1]
        return carry

    lax.fori_loop(0, n, one_block, 0)

    def finish(i, carry):
        for copy in rows_out(i):
            copy.wait()
        return carry

    lax.fori_loop(0, n, finish, 0)


def backward_kernel(block, rank_ref, bounds, *refs):
    n = 8
    a_refs, vg_refs = refs[:n], refs[n : 2 * n]
    vg_ref = vg_refs[0]
    refs = refs[n - 1 :]
    prob_ref, out_t_ref, inv_ref, stats_ref = refs[n + 1 : n + 5]
    d_refs = refs[n + 5 : 2 * n + 5]
    held, values, cot, key_t, prob, out_t_keep, stage, grad_k, grad_v, acc = refs[
        2 * n + 5 : 2 * n + 15
    ]
    sems, vg_sems, prob_sems, out_sems, d_sems = refs[2 * n + 15 :]
    rank = rank_ref[0]
    scale = 1.0 / math.sqrt(HEAD_DIM)
    width = HEADS * HEAD_DIM

    def out_in(i):
        return pltpu.make_async_copy(out_t_ref.at[i], out_t_keep.at[i], out_sems.at[i])

    prob_in = fetch_probs(n, block, bounds, prob_ref, prob, prob_sems)
    for m, ref in zip(ORDER, vg_refs):
        cot_in(ref, rank ^ m, block, cot, vg_sems).start()
        value_in(ref, rank ^ m, block, values, vg_sems).start()
    for m, ref in zip(ORDER, a_refs):
        for copy in parts_in(ref, rank ^ m, block, held, sems):
            copy.start()

    def fetch(step, carry):
        i = n - 1 - step
        out_in(i).start()
        each_slot(i, block, bounds, lambda slot: prob_in(i, slot).start())
        return carry

    lax.fori_loop(0, n, fetch, 0)
    grad_k[...] = jnp.zeros_like(grad_k)
    grad_v[...] = jnp.zeros_like(grad_v)

    def one_block(step, carry):
        i = n - 1 - step
        cot_in(vg_ref, i, block, cot, vg_sems).wait()
        out_in(i).wait()
        inv_rms = lax.rsqrt(stats_ref[0, i] / width + norm_eps)
        coef = inv_rms * inv_rms * inv_rms * stats_ref[1, i] / width
        out_t = out_t_keep[i]
        dattn_t = (inv_rms * cot[i].astype(F32).T - out_t * coef) * inv_ref[i]
        dattn_tb = dattn_t.astype(BF16)
        dattn_f = dattn_tb.astype(F32)
        delta = jnp.sum(dattn_f * out_t, axis=0, keepdims=True)
        dattn = dattn_f.T.astype(BF16)
        for first in sorted(set(FIRST_USE)):

            @pl.when(i == first)
            def _():
                for t in range(n):
                    if FIRST_USE[t] == first:
                        for copy in parts_in(a_refs[0], t, block, held, sems):
                            copy.wait()
                        value_in(vg_ref, t, block, values, vg_sems).wait()
                        cols = slice(t * block, (t + 1) * block)
                        key_t[:, cols] = held[1, cols, :].T

        own_rows = pl.ds(pl.multiple_of(i * block, block), block)
        query = held[0, own_rows, :]

        def body(near, far, masked):
            for slot in slots_of(near, far):
                prob_in(i, slot).wait()
            for number, (row, key, size, own) in enumerate(pieces(i, near, far, block)):
                rows = pl.ds(key, size)
                pb = prob[i, row : row + size, :]
                dprob = nn_dot(values[rows, :], dattn_tb)
                ds = (pb.astype(F32) * (dprob - delta)).astype(BF16)
                term = nn_dot(key_t[:, rows], ds)
                acc[...] = term if number == 0 else acc[...] + term
                grad_k[rows, :] += nn_dot(ds, query)
                grad_v[rows, :] += nn_dot(pb, dattn)

        for_each_reach(i, block, bounds, body, False)

        stage[i, 0:block, :] = (acc[...] * scale).T.astype(BF16)
        stage[i, block : 2 * block, :] = (grad_k[own_rows, :] * scale).astype(BF16)
        stage[i, 2 * block :, :] = grad_v[own_rows, :].astype(BF16)
        for m, ref in zip(ORDER, d_refs):

            @pl.when((rank ^ m) == i)
            def _():
                pltpu.make_async_copy(stage.at[i], ref, d_sems.at[m]).start()

        return carry

    lax.fori_loop(0, n, one_block, 0)
    for m, ref in zip(ORDER, d_refs):
        pltpu.make_async_copy(stage.at[0], ref, d_sems.at[m]).wait()


def pack_kernel(block, rank_ref, q_ref, k_ref, v_ref, g_ref, doc_ref, *refs):
    n = 8
    a_refs, vg_refs, sems = refs[:n], refs[n : 2 * n], refs[2 * n]
    parts = []
    for m, ref, other in zip(ORDER, a_refs, vg_refs):
        cols = pl.ds(pl.multiple_of((rank_ref[0] ^ m) * HEAD_DIM, HEAD_DIM), HEAD_DIM)
        parts.append((q_ref.at[:, cols], ref.at[0:block, :]))
        parts.append((k_ref.at[:, cols], ref.at[block : 2 * block, :]))
        parts.append((v_ref.at[:, cols], other.at[0:block, :]))
        parts.append((g_ref.at[:, cols], other.at[block:, :]))
    copies = [
        pltpu.make_async_copy(source, target, sems.at[number])
        for number, (source, target) in enumerate(parts)
    ]
    for copy in copies:
        copy.start()
    row = lax.broadcasted_iota(jnp.int32, (16, HEAD_DIM), 0)
    ids = jnp.full((16, HEAD_DIM), 4.0, F32)
    for k in range(block // HEAD_DIM):
        part = doc_ref[0:1, k * HEAD_DIM : (k + 1) * HEAD_DIM].astype(F32)
        ids = jnp.where(row == k, part, ids)
    for ref in a_refs:
        ref[2 * block :, :] = ids.astype(BF16)
    for copy in copies:
        copy.wait()


def unpack_kernel(block, rank_ref, *refs):
    n = 8
    d_refs, outs, sems = refs[:n], refs[n : n + 3], refs[n + 3]
    copies = []
    for m, ref in zip(ORDER, d_refs):
        cols = pl.ds(pl.multiple_of((rank_ref[0] ^ m) * HEAD_DIM, HEAD_DIM), HEAD_DIM)
        for part, out in enumerate(outs):
            rows = slice(part * block, (part + 1) * block)
            copies.append(
                pltpu.make_async_copy(ref.at[rows, :], out.at[:, cols], sems.at[len(copies)])
            )
    for copy in copies:
        copy.start()
    for copy in copies:
        copy.wait()


def normed_kernel(block, stats_ref, home_ref, out_ref):
    inv_rms = lax.rsqrt(stats_ref[...] / (HEADS * HEAD_DIM) + norm_eps)
    spread = jnp.broadcast_to(inv_rms, (HEAD_DIM, block)).T
    for h in range(home_ref.shape[0]):
        cols = slice(h * HEAD_DIM, (h + 1) * HEAD_DIM)
        out_ref[:, cols] = (home_ref[h].astype(F32) * spread).astype(BF16)


SMEM_SPEC = pl.BlockSpec(memory_space=pltpu.SMEM)
ANY_SPEC = pl.BlockSpec(memory_space=pl.ANY)
VMEM_SPEC = pl.BlockSpec(memory_space=pltpu.VMEM)


def shape_of(shape, dtype):
    return jax.ShapeDtypeStruct(shape, dtype)


def swap(value, m):
    if m == 0:
        return value
    n = lax.axis_size("seq")
    return lax.ppermute(value, "seq", [(s, s ^ m) for s in range(n)])


def swap_all(parts):
    return [swap(part, m) for m, part in zip(ORDER, parts)]


def all_to_all(value):
    return lax.all_to_all(value, "seq", split_axis=0, concat_axis=0, tiled=True)


def sum_everywhere(stats):
    stats = stats + swap(stats, 1)
    stats = stats + swap(stats, 2) + swap(stats, 4) + swap(stats, 6)
    heads = lax.axis_size("head")
    parts = [
        lax.ppermute(stats, "head", [(s, (s + d) % heads) for s in range(heads)])
        for d in range(1, heads)
    ]
    return functools.reduce(jnp.add, parts, stats)


def params():
    return pltpu.CompilerParams(vmem_limit_bytes=VMEM_BYTES)


def run_score(rank, a, block):
    n = len(a)
    return pl.pallas_call(
        functools.partial(score_kernel, block),
        out_shape=[
            shape_of((n, 4 * block, block), BF16),
            shape_of((n, 1, block), F32),
            shape_of((3,), jnp.int32),
        ],
        in_specs=[SMEM_SPEC] + [ANY_SPEC] * n,
        out_specs=[ANY_SPEC, VMEM_SPEC, SMEM_SPEC],
        scratch_shapes=[
            pltpu.VMEM((2, n * block, HEAD_DIM), BF16),
            pltpu.VMEM((n, 16, HEAD_DIM), BF16),
            pltpu.VMEM((n, 4 * block, block), BF16),
            pltpu.SemaphoreType.DMA((2, n)),
            pltpu.SemaphoreType.DMA((n,)),
            pltpu.SemaphoreType.DMA((n, 4)),
        ],
        compiler_params=params(),
        name="score",
    )(rank, *a)


def run_attend(rank, bounds, vg, probs, inv_total, block):
    n = len(vg)
    return pl.pallas_call(
        functools.partial(attend_kernel, block),
        out_shape=[
            shape_of((n, HEAD_DIM, block), F32),
            shape_of((n, block, HEAD_DIM), BF16),
            shape_of((2, n, 1, block), F32),
        ],
        in_specs=[SMEM_SPEC] * 2 + [ANY_SPEC] * (n + 1) + [VMEM_SPEC],
        out_specs=[ANY_SPEC] * 2 + [VMEM_SPEC],
        scratch_shapes=[
            pltpu.VMEM((n * block, HEAD_DIM), BF16),
            pltpu.VMEM((n, block, HEAD_DIM), BF16),
            pltpu.VMEM((HEAD_DIM, n * block), BF16),
            pltpu.VMEM((n, 4 * block, block), BF16),
            pltpu.VMEM((n, HEAD_DIM, block), F32),
            pltpu.VMEM((n, block, HEAD_DIM), BF16),
            pltpu.VMEM((HEAD_DIM, block), F32),
            pltpu.SemaphoreType.DMA((2, n)),
            pltpu.SemaphoreType.DMA((n, 4)),
            pltpu.SemaphoreType.DMA((2, n)),
        ],
        compiler_params=params(),
        name="attend",
    )(rank, bounds, *vg, probs, inv_total)


def run_backward(rank, bounds, a, vg, probs, out_t, inv_total, stats, block):
    n = len(a)
    return pl.pallas_call(
        functools.partial(backward_kernel, block),
        out_shape=[shape_of((3 * block, HEAD_DIM), BF16)] * n,
        in_specs=[SMEM_SPEC] * 2 + [ANY_SPEC] * (2 * n + 2) + [VMEM_SPEC] * 2,
        out_specs=[ANY_SPEC] * n,
        scratch_shapes=[
            pltpu.VMEM((2, n * block, HEAD_DIM), BF16),
            pltpu.VMEM((n * block, HEAD_DIM), BF16),
            pltpu.VMEM((n, block, HEAD_DIM), BF16),
            pltpu.VMEM((HEAD_DIM, n * block), BF16),
            pltpu.VMEM((n, 4 * block, block), BF16),
            pltpu.VMEM((n, HEAD_DIM, block), F32),
            pltpu.VMEM((n, 3 * block, HEAD_DIM), BF16),
            pltpu.VMEM((n * block, HEAD_DIM), F32),
            pltpu.VMEM((n * block, HEAD_DIM), F32),
            pltpu.VMEM((HEAD_DIM, block), F32),
            pltpu.SemaphoreType.DMA((2, n)),
            pltpu.SemaphoreType.DMA((2, n)),
            pltpu.SemaphoreType.DMA((n, 4)),
            pltpu.SemaphoreType.DMA((n,)),
            pltpu.SemaphoreType.DMA((n,)),
        ],
        compiler_params=params(),
        name="backward",
    )(rank, bounds, *a, *vg, probs, out_t, inv_total, stats)


def by_head(queries, keys, values, grad_normed, docs):
    block, width_dev = queries.shape
    n = width_dev // HEAD_DIM
    rank = lax.axis_index("seq").reshape(1).astype(jnp.int32)
    packed = pl.pallas_call(
        functools.partial(pack_kernel, block),
        out_shape=[shape_of((2 * block + 16, HEAD_DIM), BF16)] * n
        + [shape_of((2 * block, HEAD_DIM), BF16)] * n,
        in_specs=[SMEM_SPEC] + [ANY_SPEC] * 4 + [VMEM_SPEC],
        out_specs=[VMEM_SPEC] * (2 * n),
        scratch_shapes=[pltpu.SemaphoreType.DMA((4 * n,))],
        compiler_params=params(),
        name="pack",
    )(rank, queries, keys, values, grad_normed, docs.reshape(1, block))
    a = swap_all(packed[:n])
    a[1:TIE], vg = lax.optimization_barrier((a[1:TIE], list(packed[n:])))
    vg = swap_all(vg)

    probs, inv_total, bounds = run_score(rank, a, block)
    out_t, out, stats = run_attend(rank, bounds, vg, probs, inv_total, block)
    stats = sum_everywhere(stats.reshape(2, n * block)).reshape(2, n, 1, block)

    home = all_to_all(out)
    grads = run_backward(rank, bounds, a, vg, probs, out_t, inv_total, stats, block)
    home, grads = lax.optimization_barrier((home, grads))
    own_stats = lax.dynamic_index_in_dim(stats[0], rank[0], 0, keepdims=False)
    normed = pl.pallas_call(
        functools.partial(normed_kernel, block),
        out_shape=shape_of((block, width_dev), BF16),
        in_specs=[VMEM_SPEC] * 2,
        out_specs=VMEM_SPEC,
        compiler_params=params(),
        name="normed",
    )(own_stats, home)
    back = swap_all(grads)
    grad_outs = pl.pallas_call(
        functools.partial(unpack_kernel, block),
        out_shape=[shape_of((block, width_dev), BF16)] * 3,
        in_specs=[SMEM_SPEC] + [ANY_SPEC] * n,
        out_specs=[VMEM_SPEC] * 3,
        scratch_shapes=[pltpu.SemaphoreType.DMA((3 * n,))],
        compiler_params=params(),
        name="unpack",
    )(rank, *back)
    return (normed, *grad_outs)


def from_behind(value, axis, steps):
    count = lax.axis_size(axis)
    initial, last = (max(0, -steps), min(count, count - steps))
    return lax.ppermute(value, axis, [(source, source + steps) for source in range(initial, last)])


def allowed_pairs(all_docs, own_docs, query_pos, seq_rank, offset, block_len):
    key_start = (seq_rank - offset) * block_len
    key_pos = key_start + jnp.arange(block_len, dtype=jnp.int32)
    key_docs = lax.dynamic_slice_in_dim(all_docs, jnp.maximum(key_start, 0), block_len)
    return (
        (key_pos[None, :] >= 0)
        & (key_pos[None, :] <= query_pos[:, None])
        & (key_docs[None, :] == own_docs[:, None])
    )


def masked_scores(query_heads, source, allowed, score_scale):
    key_heads = source[0].reshape(query_heads.shape)
    scores = (
        jnp.einsum("qhd,khd->hqk", query_heads, key_heads, preferred_element_type=jnp.float32)
        * score_scale
    )
    return jnp.where(allowed[None], scores, -jnp.inf)


def by_block(queries, keys, values, grad_normed, docs):
    block_len, width_dev = queries.shape
    heads_dev = width_dev // HEAD_DIM
    width = HEADS * HEAD_DIM
    score_scale = 1.0 / math.sqrt(HEAD_DIM)
    seq_rank = lax.axis_index("seq")
    levels = lax.axis_size("seq").bit_length() - 1
    distances = [2**exponent for exponent in range(levels)]
    all_docs = lax.all_gather(docs, "seq", axis=0, tiled=True)
    query_pos = seq_rank * block_len + jnp.arange(block_len, dtype=jnp.int32)
    query_heads = queries.reshape(block_len, heads_dev, HEAD_DIM)
    key_value = jnp.stack([keys, values])
    fetched = [from_behind(key_value, "seq", offset) for offset in distances]
    offsets = [0] + distances
    sources = [key_value] + fetched
    masks = [
        allowed_pairs(all_docs, docs, query_pos, seq_rank, offset, block_len) for offset in offsets
    ]
    shape_heads = (block_len, heads_dev, HEAD_DIM)
    row_max = jnp.full((heads_dev, block_len), -jnp.inf, jnp.float32)
    row_sum = jnp.zeros((heads_dev, block_len), jnp.float32)
    for source, allowed in zip(sources, masks):

        def update_stats(state, source_kv, allowed_now):
            old_max, old_sum = state
            scores = masked_scores(query_heads, source_kv, allowed_now, score_scale)
            new_max = jnp.maximum(old_max, jnp.max(scores, axis=-1))
            new_sum = old_sum * jnp.exp(old_max - new_max) + jnp.sum(
                jnp.exp(scores - new_max[..., None]), axis=-1
            )
            return (new_max, new_sum)

        def keep_stats(state, source_kv, allowed_now):
            return state

        row_max, row_sum = lax.cond(
            jnp.any(allowed), update_stats, keep_stats, (row_max, row_sum), source, allowed
        )
    log_total = row_max + jnp.log(row_sum)
    attn = jnp.zeros(shape_heads, jnp.float32)
    for source, allowed in zip(sources, masks):

        def forward_term(source_kv, allowed_now):
            scores = masked_scores(query_heads, source_kv, allowed_now, score_scale)
            prob_round = jnp.exp(scores - log_total[..., None]).astype(jnp.bfloat16)
            value_heads = source_kv[1].reshape(shape_heads)
            return jnp.einsum(
                "hqk,khd->qhd", prob_round, value_heads, preferred_element_type=jnp.float32
            )

        def empty_term(source_kv, allowed_now):
            return jnp.zeros(shape_heads, jnp.float32)

        attn = attn + lax.cond(jnp.any(allowed), forward_term, empty_term, source, allowed)
    attn_flat = attn.reshape(block_len, width_dev)
    cotangent = grad_normed.astype(jnp.float32)
    square_local = jnp.sum(attn_flat * attn_flat, axis=-1)
    square_total = lax.psum(square_local, "head")
    inv_rms = lax.rsqrt(square_total / width + norm_eps)
    normed = (attn_flat * inv_rms[:, None]).astype(jnp.bfloat16)
    projection = lax.psum(jnp.sum(cotangent * attn_flat, axis=-1), "head")
    dattn = (
        inv_rms[:, None] * cotangent - attn_flat * (inv_rms**3 * projection / width)[:, None]
    ).astype(jnp.bfloat16)
    dattn_heads = dattn.reshape(shape_heads)
    row_delta = jnp.sum(dattn_heads.astype(jnp.float32) * attn, axis=-1).T
    grad_query = jnp.zeros(shape_heads, jnp.float32)
    partials = []
    for source, allowed in zip(sources, masks):

        def backward_term(source_kv, allowed_now):
            scores = masked_scores(query_heads, source_kv, allowed_now, score_scale)
            prob_exact = jnp.exp(scores - log_total[..., None])
            prob_round = prob_exact.astype(jnp.bfloat16)
            key_heads = source_kv[0].reshape(shape_heads)
            value_heads = source_kv[1].reshape(shape_heads)
            dprob = jnp.einsum(
                "qhd,khd->hqk", dattn_heads, value_heads, preferred_element_type=jnp.float32
            )
            dscore = (prob_exact * (dprob - row_delta[..., None]) * score_scale).astype(
                jnp.bfloat16
            )
            query_term = jnp.einsum(
                "hqk,khd->qhd", dscore, key_heads, preferred_element_type=jnp.float32
            )
            key_term = jnp.einsum(
                "hqk,qhd->khd", dscore, query_heads, preferred_element_type=jnp.float32
            )
            value_term = jnp.einsum(
                "hqk,qhd->khd", prob_round, dattn_heads, preferred_element_type=jnp.float32
            )
            return (
                query_term,
                jnp.stack(
                    [
                        key_term.reshape(block_len, width_dev),
                        value_term.reshape(block_len, width_dev),
                    ]
                ),
            )

        def empty_pair(source_kv, allowed_now):
            return (
                jnp.zeros(shape_heads, jnp.float32),
                jnp.zeros((2, block_len, width_dev), jnp.float32),
            )

        query_term, pair_term = lax.cond(
            jnp.any(allowed), backward_term, empty_pair, source, allowed
        )
        grad_query = grad_query + query_term
        partials.append(pair_term)
    local_term = partials[0]
    far_terms = partials[1:]
    summed = local_term
    for offset, addend in zip(distances, far_terms):
        summed = summed + from_behind(addend.astype(jnp.bfloat16), "seq", -offset).astype(
            addend.dtype
        )
    grad_queries = grad_query.reshape(block_len, width_dev).astype(jnp.bfloat16)
    return (normed, grad_queries, summed[0].astype(jnp.bfloat16), summed[1].astype(jnp.bfloat16))


def body(queries, *others):
    block_len, width_dev = queries.shape
    if lax.axis_size("seq") == 8 and width_dev == 8 * HEAD_DIM and block_len == 512:
        return by_head(queries, *others)
    return by_block(queries, *others)


def solution(mesh):
    placed = (P("seq", "head"), P("seq", "head"), P("seq", "head"), P("seq", "head"), P("seq"))
    return jax.shard_map(
        body,
        mesh=mesh,
        in_specs=placed,
        out_specs=(P("seq", "head"), P("seq", "head"), P("seq", "head"), P("seq", "head")),
        check_vma=False,
    )
```

```python
import functools
import math

import jax
import jax.numpy as jnp
from jax import lax
from jax.experimental import pallas as pl
from jax.experimental.pallas import tpu as pltpu
from jax.sharding import PartitionSpec as P

HEADS = 32
HEAD_DIM = 128


norm_eps = 1e-06

OFFSETS = (0, 1, 2, 4)
NEG = -1e30
F32 = jnp.float32
BF16 = jnp.bfloat16
VMEM_BYTES = 60 * 1024 * 1024


ORDER = (0, 1, 2, 4, 6, 3, 5, 7)
TIE = 3
FIRST_USE = [max(t + off for off in OFFSETS if t + off < 8) for t in range(8)]


def find_bounds(ids, bounds):
    ids = ids[...].astype(F32)
    for d in range(3):
        count = jnp.sum(jnp.where(ids < d + 0.5, 1.0, 0.0))
        bounds[d] = count.astype(jnp.int32)


def doc_of(position, bounds):
    doc = jnp.int32(0)
    for d in range(3):
        doc = doc + (position >= bounds[d]).astype(jnp.int32)
    return doc


def reach(i, block, bounds):
    first, last = doc_of(i * block, bounds), doc_of(i * block + block - 1, bounds)

    def active(off):
        return (i >= off) & (first == doc_of((i - off + 1) * block - 1, bounds))

    def full(off):
        return doc_of((i - off) * block, bounds) == last

    near = 1 + active(1).astype(jnp.int32) + active(2).astype(jnp.int32)
    return near, active(4), full(2), full(4)


def pieces(i, near, far, block):
    found = []
    if far:
        found.append((0, (i - 4) * block, block, False))
    if near > 1:
        found.append(((4 - near) * block, (i - near + 1) * block, (near - 1) * block, False))
    found.append((3 * block, i * block, block, True))
    return [(row, pl.multiple_of(key, block), size, own) for row, key, size, own in found]


def slots_of(near, far):
    return ([0] if far else []) + list(range(4 - near, 4))


def for_each_reach(i, block, bounds, body, split_full):
    near, far, full2, full4 = reach(i, block, bounds)
    pl.when(near == 1)(functools.partial(body, 1, False, True))
    pl.when(near == 2)(functools.partial(body, 2, False, True))
    alone = (near == 3) & jnp.logical_not(far)
    if not split_full:
        pl.when(alone)(functools.partial(body, 3, False, True))
        pl.when(far)(functools.partial(body, 3, True, True))
        return
    pl.when(alone & full2)(functools.partial(body, 3, False, False))
    pl.when(alone & jnp.logical_not(full2))(functools.partial(body, 3, False, True))
    pl.when(far & full4)(functools.partial(body, 3, True, False))
    pl.when(far & jnp.logical_not(full4))(functools.partial(body, 3, True, True))


def each_slot(i, block, bounds, act):
    near, far, _, _ = reach(i, block, bounds)
    act(3)
    pl.when(near > 1)(lambda: act(2))
    pl.when(near > 2)(lambda: act(1))
    pl.when(far)(lambda: act(0))


def by_rows(i, act):
    if isinstance(i, int):
        act(0 if i >= 4 else max(1, 3 - i))
        return
    pl.when(i == 0)(lambda: act(3))
    pl.when(i == 1)(lambda: act(2))
    pl.when((i == 2) | (i == 3))(lambda: act(1))
    pl.when(i >= 4)(lambda: act(0))


def move_probs(source, target, sems, block, i, slot):
    rows = slice(slot * block, 4 * block)
    return pltpu.make_async_copy(source.at[i, rows, :], target.at[i, rows, :], sems.at[i])


def doc_starts(i, block, bounds):
    pos = i * block + lax.broadcasted_iota(jnp.int32, (1, block), 1)
    start = jnp.zeros((1, block), jnp.int32)
    for d in range(3):
        start = jnp.where(pos >= bounds[d], jnp.maximum(start, bounds[d]), start)
    return pos, start


def nt_dot(a, b):
    return lax.dot_general(a, b, (((1,), (1,)), ((), ())), preferred_element_type=F32)


def nn_dot(a, b):
    return lax.dot_general(a, b, (((1,), (0,)), ((), ())), preferred_element_type=F32)


def parts_in(ref, t, block, held, sems):
    return [
        pltpu.make_async_copy(
            ref.at[part * block : (part + 1) * block, :],
            held.at[part, pl.ds(pl.multiple_of(t * block, block), block), :],
            sems.at[part, t],
        )
        for part in range(2)
    ]


def score_kernel(block, rank_ref, *refs):
    n = 8
    a_refs = refs[:n]
    prob_ref, inv_ref, bounds = refs[n : n + 3]
    held, ids, prob, sems, id_sems, prob_sems = refs[n + 3 :]
    rank = rank_ref[0]

    def ids_in(m, ref):
        return pltpu.make_async_copy(ref.at[2 * block :, :], ids.at[rank ^ m], id_sems.at[m])

    for m, ref in zip(ORDER, a_refs):
        ids_in(m, ref).start()
    for m, ref in zip(ORDER, a_refs):
        for copy in parts_in(ref, rank ^ m, block, held, sems):
            copy.start()
    for m, ref in zip(ORDER, a_refs):
        ids_in(m, ref).wait()
    find_bounds(ids, bounds)

    gain = math.log2(math.e) / math.sqrt(HEAD_DIM)

    prob_out = functools.partial(move_probs, prob, prob_ref, prob_sems, block)

    def one_block(i, carry):
        own_rows = pl.ds(pl.multiple_of(i * block, block), block)
        for copy in parts_in(a_refs[0], i, block, held, sems):
            copy.wait()
        query = held[0, own_rows, :]
        q_pos, q_start = doc_starts(i, block, bounds)

        def body(near, far, masked):
            found = pieces(i, near, far, block)
            scores, top = [], None
            for row, key, size, own in found:
                s = nt_dot(held[1, pl.ds(key, size), :], query) * gain
                if masked or own:
                    k_pos = key + lax.broadcasted_iota(jnp.int32, (size, 1), 0)
                    if not masked:
                        keep = k_pos <= q_pos
                    elif own:
                        keep = (k_pos >= q_start) & (k_pos <= q_pos)
                    else:
                        keep = k_pos >= q_start
                    s = jnp.where(keep, s, NEG)
                scores.append(s)
                peak = jnp.max(s, axis=0, keepdims=True)
                top = peak if top is None else jnp.maximum(top, peak)
            total = None
            for (row, key, size, own), s in zip(found, scores):
                p = jnp.exp2(s - top)
                line = jnp.sum(p, axis=0, keepdims=True)
                prob[i, row : row + size, :] = p.astype(BF16)
                total = line if total is None else total + line
            inv_ref[i] = 1.0 / total

        for_each_reach(i, block, bounds, body, True)
        by_rows(i, lambda slot: prob_out(i, slot).start())
        return carry

    lax.fori_loop(0, n, one_block, 0)

    for i in range(n):
        by_rows(i, lambda slot: prob_out(i, slot).wait())


def value_in(vg_ref, t, block, values, sems):
    return pltpu.make_async_copy(
        vg_ref.at[0:block, :],
        values.at[pl.ds(pl.multiple_of(t * block, block), block), :],
        sems.at[0, t],
    )


def cot_in(vg_ref, t, block, cot, sems):
    return pltpu.make_async_copy(vg_ref.at[block:, :], cot.at[t], sems.at[1, t])


def attend_kernel(block, rank_ref, bounds, *refs):
    n = 8
    vg_refs = refs[:n]
    prob_ref, inv_ref, out_t_ref, out_ref, stats_ref = refs[n : n + 5]
    values, cot, val_t, prob, out_t_keep, out_keep, acc, vg_sems, prob_sems, out_sems = refs[n + 5 :]
    vg_ref = vg_refs[0]
    prob_in = functools.partial(move_probs, prob_ref, prob, prob_sems, block)

    def rows_out(i):
        return (
            pltpu.make_async_copy(out_t_keep.at[i], out_t_ref.at[i], out_sems.at[0, i]),
            pltpu.make_async_copy(out_keep.at[i], out_ref.at[i], out_sems.at[1, i]),
        )

    for m, ref in zip(ORDER, vg_refs):
        value_in(ref, rank_ref[0] ^ m, block, values, vg_sems).start()
        cot_in(ref, rank_ref[0] ^ m, block, cot, vg_sems).start()
    for t in range(n):
        by_rows(t, lambda slot: prob_in(t, slot).start())
    ones = jnp.ones((16, HEAD_DIM), BF16)

    def one_block(i, carry):
        own_rows = pl.ds(pl.multiple_of(i * block, block), block)
        value_in(vg_ref, i, block, values, vg_sems).wait()
        val_t[:, own_rows] = values[own_rows, :].T

        def body(near, far, masked):
            out = None
            for row, key, size, own in pieces(i, near, far, block):
                term = nn_dot(val_t[:, pl.ds(key, size)], prob[i, row : row + size, :])
                out = term if out is None else out + term
            acc[...] = out

        by_rows(i, lambda slot: prob_in(i, slot).wait())
        for_each_reach(i, block, bounds, body, False)

        out_t = acc[...] * inv_ref[i]
        out_t_keep[i] = out_t
        rows_out(i)[0].start()
        stats_ref[0:1, own_rows] = jnp.sum(out_t * out_t, axis=0, keepdims=True)
        return carry

    lax.fori_loop(0, n, one_block, 0)

    for i in range(n):
        cols = slice(i * block, (i + 1) * block)
        out = out_t_keep[i].T
        out_keep[i] = out.astype(BF16)
        rows_out(i)[1].start()
        cot_in(vg_ref, i, block, cot, vg_sems).wait()
        x = cot[i].astype(F32) * out
        high = x.astype(BF16)
        low = (x - high.astype(F32)).astype(BF16)
        stats_ref[1:2, cols] = (nt_dot(ones, high) + nt_dot(ones, low))[0:1]

    def finish(i, carry):
        for copy in rows_out(i):
            copy.wait()
        return carry

    lax.fori_loop(0, n, finish, 0)


def backward_kernel(block, rank_ref, bounds, *refs):
    n = 8
    a_refs, vg_refs = refs[:n], refs[n : 2 * n]
    vg_ref = vg_refs[0]
    refs = refs[n - 1 :]
    prob_ref, out_t_ref, inv_ref, stats_ref = refs[n + 1 : n + 5]
    d_refs = refs[n + 5 : 2 * n + 5]
    held, values, cot, key_t, prob, out_t_keep, stage, grad_k, grad_v, acc = refs[
        2 * n + 5 : 2 * n + 15
    ]
    dattn_t, dattn_keep, deltas = refs[2 * n + 15 : 2 * n + 18]
    sems, vg_sems, prob_sems, out_sems, d_sems = refs[2 * n + 18 :]
    rank = rank_ref[0]
    scale = 1.0 / math.sqrt(HEAD_DIM)
    width = HEADS * HEAD_DIM

    def out_in(i):
        return pltpu.make_async_copy(out_t_ref.at[i], out_t_keep.at[i], out_sems.at[i])

    def prob_in(i, slot):
        rows = slice(slot * block, (slot + 1) * block)
        return pltpu.make_async_copy(
            prob_ref.at[i, rows, :], prob.at[i, rows, :], prob_sems.at[i, slot]
        )

    for m, ref in zip(ORDER, vg_refs):
        cot_in(ref, rank ^ m, block, cot, vg_sems).start()
    for i in reversed(range(n)):
        out_in(i).start()
    for m, ref in zip(ORDER, vg_refs):
        value_in(ref, rank ^ m, block, values, vg_sems).start()
    for m, ref in zip(ORDER, a_refs):
        for copy in parts_in(ref, rank ^ m, block, held, sems):
            copy.start()

    def fetch(step, carry):
        i = n - 1 - step
        each_slot(i, block, bounds, lambda slot: prob_in(i, slot).start())
        return carry

    lax.fori_loop(0, n, fetch, 0)
    grad_k[...] = jnp.zeros_like(grad_k)
    grad_v[...] = jnp.zeros_like(grad_v)

    for i in reversed(range(n)):
        cols = slice(i * block, (i + 1) * block)
        cot_in(vg_ref, i, block, cot, vg_sems).wait()
        out_in(i).wait()
        inv_rms = lax.rsqrt(stats_ref[0:1, cols] / width + norm_eps)
        coef = inv_rms * inv_rms * inv_rms * stats_ref[1:2, cols] / width
        out_t = out_t_keep[i]
        rows_t = (inv_rms * cot[i].astype(F32).T - out_t * coef) * inv_ref[i]
        rounded = rows_t.astype(BF16)
        dattn_t[:, cols] = rounded
        rows_f = rounded.astype(F32)
        deltas[0:1, cols] = jnp.sum(rows_f * out_t, axis=0, keepdims=True)
        dattn_keep[cols, :] = rows_f.T.astype(BF16)

    def one_block(step, carry):
        i = n - 1 - step
        own_rows = pl.ds(pl.multiple_of(i * block, block), block)
        dattn_tb = dattn_t[:, own_rows]
        dattn = dattn_keep[own_rows, :]
        delta = deltas[0:1, own_rows]
        for first in sorted(set(FIRST_USE)):

            @pl.when(i == first)
            def _():
                for t in range(n):
                    if FIRST_USE[t] == first:
                        for copy in parts_in(a_refs[0], t, block, held, sems):
                            copy.wait()
                        value_in(vg_ref, t, block, values, vg_sems).wait()
                        cols = slice(t * block, (t + 1) * block)
                        key_t[:, cols] = held[1, cols, :].T

        query = held[0, own_rows, :]

        def body(near, far, masked):
            for slot in slots_of(near, far):
                prob_in(i, slot).wait()
            for number, (row, key, size, own) in enumerate(pieces(i, near, far, block)):
                rows = pl.ds(key, size)
                pb = prob[i, row : row + size, :]
                dprob = nn_dot(values[rows, :], dattn_tb)
                ds = (pb.astype(F32) * (dprob - delta)).astype(BF16)
                term = nn_dot(key_t[:, rows], ds)
                acc[...] = term if number == 0 else acc[...] + term
                grad_k[rows, :] += nn_dot(ds, query)
                grad_v[rows, :] += nn_dot(pb, dattn)

        for_each_reach(i, block, bounds, body, False)

        stage[i, 0:block, :] = (acc[...] * scale).T.astype(BF16)
        stage[i, block : 2 * block, :] = (grad_k[own_rows, :] * scale).astype(BF16)
        stage[i, 2 * block :, :] = grad_v[own_rows, :].astype(BF16)
        for m, ref in zip(ORDER, d_refs):

            @pl.when((rank ^ m) == i)
            def _():
                pltpu.make_async_copy(stage.at[i], ref, d_sems.at[m]).start()

        return carry

    lax.fori_loop(0, n, one_block, 0)
    for m, ref in zip(ORDER, d_refs):
        pltpu.make_async_copy(stage.at[0], ref, d_sems.at[m]).wait()


def own_cols(rank_ref, m):
    return pl.ds(pl.multiple_of((rank_ref[0] ^ m) * HEAD_DIM, HEAD_DIM), HEAD_DIM)


def start_all(pairs, sems):
    copies = [
        pltpu.make_async_copy(source, target, sems.at[number])
        for number, (source, target) in enumerate(pairs)
    ]
    for copy in copies:
        copy.start()
    return copies


def pass_on(arrivals, keep, refs, sems):
    copies = []
    for index, ref in enumerate(refs):
        for copy in arrivals[index]:
            copy.wait()
        copies.append(pltpu.make_async_copy(keep.at[index], ref, sems.at[index]))
        copies[-1].start()
    for copy in copies:
        copy.wait()


def gather_columns(block, rank_ref, top_ref, low_ref, keep, sems):
    arrivals = []
    for index, m in enumerate(ORDER):
        cols = own_cols(rank_ref, m)
        pairs = [
            (top_ref.at[:, cols], keep.at[index, 0:block, :]),
            (low_ref.at[:, cols], keep.at[index, block : 2 * block, :]),
        ]
        arrivals.append(start_all(pairs, sems.at[index]))
    return arrivals


def pack_scores_kernel(block, rank_ref, q_ref, k_ref, doc_ref, *refs):
    n = 8
    a_refs, keep, sems, out_sems = refs[:n], *refs[n:]
    arrivals = gather_columns(block, rank_ref, q_ref, k_ref, keep, sems)
    row = lax.broadcasted_iota(jnp.int32, (16, HEAD_DIM), 0)
    ids = jnp.full((16, HEAD_DIM), 4.0, F32)
    for k in range(block // HEAD_DIM):
        part = doc_ref[0:1, k * HEAD_DIM : (k + 1) * HEAD_DIM].astype(F32)
        ids = jnp.where(row == k, part, ids)
    for index in range(n):
        keep[index, 2 * block :, :] = ids.astype(BF16)
    pass_on(arrivals, keep, a_refs, out_sems)


def pack_values_kernel(block, rank_ref, v_ref, g_ref, *refs):
    n = 8
    vg_refs, keep, sems, out_sems = refs[:n], *refs[n:]
    pass_on(gather_columns(block, rank_ref, v_ref, g_ref, keep, sems), keep, vg_refs, out_sems)


def unpack_kernel(block, rank_ref, *refs):
    n = 8
    d_refs, outs, keep, sems, out_sems = refs[:n], refs[n : n + 3], *refs[n + 3 :]
    arrivals = []
    for part in range(3):
        rows = slice(part * block, (part + 1) * block)
        pairs = [
            (ref.at[rows, :], keep.at[part, :, own_cols(rank_ref, m)])
            for m, ref in zip(ORDER, d_refs)
        ]
        arrivals.append(start_all(pairs, sems.at[part]))
    copies = []
    for part, out in enumerate(outs):
        for copy in arrivals[part]:
            copy.wait()
        copies.append(pltpu.make_async_copy(keep.at[part], out, out_sems.at[part]))
        copies[-1].start()
    for copy in copies:
        copy.wait()


def normed_kernel(block, rank_ref, stats_ref, home_ref, out_ref):
    own_rows = pl.ds(pl.multiple_of(rank_ref[0] * block, block), block)
    inv_rms = lax.rsqrt(stats_ref[0:1, own_rows] / (HEADS * HEAD_DIM) + norm_eps)
    spread = jnp.broadcast_to(inv_rms, (HEAD_DIM, block)).T
    for h in range(home_ref.shape[0]):
        cols = slice(h * HEAD_DIM, (h + 1) * HEAD_DIM)
        out_ref[:, cols] = (home_ref[h].astype(F32) * spread).astype(BF16)


SMEM_SPEC = pl.BlockSpec(memory_space=pltpu.SMEM)
ANY_SPEC = pl.BlockSpec(memory_space=pl.ANY)
VMEM_SPEC = pl.BlockSpec(memory_space=pltpu.VMEM)


def shape_of(shape, dtype):
    return jax.ShapeDtypeStruct(shape, dtype)


def swap(value, m):
    if m == 0:
        return value
    n = lax.axis_size("seq")
    return lax.ppermute(value, "seq", [(s, s ^ m) for s in range(n)])


def swap_all(parts):
    return [swap(part, m) for m, part in zip(ORDER, parts)]


def all_to_all(value):
    return lax.all_to_all(value, "seq", split_axis=0, concat_axis=0, tiled=True)


def sum_everywhere(stats):
    stats = stats + swap(stats, 1)
    stats = stats + swap(stats, 2) + swap(stats, 4) + swap(stats, 6)
    heads = lax.axis_size("head")
    parts = [
        lax.ppermute(stats, "head", [(s, (s + d) % heads) for s in range(heads)])
        for d in range(1, heads)
    ]
    return functools.reduce(jnp.add, parts, stats)


def params():
    return pltpu.CompilerParams(vmem_limit_bytes=VMEM_BYTES)


def run_score(rank, a, block):
    n = len(a)
    return pl.pallas_call(
        functools.partial(score_kernel, block),
        out_shape=[
            shape_of((n, 4 * block, block), BF16),
            shape_of((n, 1, block), F32),
            shape_of((3,), jnp.int32),
        ],
        in_specs=[SMEM_SPEC] + [ANY_SPEC] * n,
        out_specs=[ANY_SPEC, VMEM_SPEC, SMEM_SPEC],
        scratch_shapes=[
            pltpu.VMEM((2, n * block, HEAD_DIM), BF16),
            pltpu.VMEM((n, 16, HEAD_DIM), BF16),
            pltpu.VMEM((n, 4 * block, block), BF16),
            pltpu.SemaphoreType.DMA((2, n)),
            pltpu.SemaphoreType.DMA((n,)),
            pltpu.SemaphoreType.DMA((n,)),
        ],
        compiler_params=params(),
        name="score",
    )(rank, *a)


def run_attend(rank, bounds, vg, probs, inv_total, block):
    n = len(vg)
    return pl.pallas_call(
        functools.partial(attend_kernel, block),
        out_shape=[
            shape_of((n, HEAD_DIM, block), F32),
            shape_of((n, block, HEAD_DIM), BF16),
            shape_of((2, n * block), F32),
        ],
        in_specs=[SMEM_SPEC] * 2 + [ANY_SPEC] * (n + 1) + [VMEM_SPEC],
        out_specs=[ANY_SPEC] * 2 + [VMEM_SPEC],
        scratch_shapes=[
            pltpu.VMEM((n * block, HEAD_DIM), BF16),
            pltpu.VMEM((n, block, HEAD_DIM), BF16),
            pltpu.VMEM((HEAD_DIM, n * block), BF16),
            pltpu.VMEM((n, 4 * block, block), BF16),
            pltpu.VMEM((n, HEAD_DIM, block), F32),
            pltpu.VMEM((n, block, HEAD_DIM), BF16),
            pltpu.VMEM((HEAD_DIM, block), F32),
            pltpu.SemaphoreType.DMA((2, n)),
            pltpu.SemaphoreType.DMA((n,)),
            pltpu.SemaphoreType.DMA((2, n)),
        ],
        compiler_params=params(),
        name="attend",
    )(rank, bounds, *vg, probs, inv_total)


def run_backward(rank, bounds, a, vg, probs, out_t, inv_total, stats, block):
    n = len(a)
    return pl.pallas_call(
        functools.partial(backward_kernel, block),
        out_shape=[shape_of((3 * block, HEAD_DIM), BF16)] * n,
        in_specs=[SMEM_SPEC] * 2 + [ANY_SPEC] * (2 * n + 2) + [VMEM_SPEC] * 2,
        out_specs=[ANY_SPEC] * n,
        scratch_shapes=[
            pltpu.VMEM((2, n * block, HEAD_DIM), BF16),
            pltpu.VMEM((n * block, HEAD_DIM), BF16),
            pltpu.VMEM((n, block, HEAD_DIM), BF16),
            pltpu.VMEM((HEAD_DIM, n * block), BF16),
            pltpu.VMEM((n, 4 * block, block), BF16),
            pltpu.VMEM((n, HEAD_DIM, block), F32),
            pltpu.VMEM((n, 3 * block, HEAD_DIM), BF16),
            pltpu.VMEM((n * block, HEAD_DIM), F32),
            pltpu.VMEM((n * block, HEAD_DIM), F32),
            pltpu.VMEM((HEAD_DIM, block), F32),
            pltpu.VMEM((HEAD_DIM, n * block), BF16),
            pltpu.VMEM((n * block, HEAD_DIM), BF16),
            pltpu.VMEM((1, n * block), F32),
            pltpu.SemaphoreType.DMA((2, n)),
            pltpu.SemaphoreType.DMA((2, n)),
            pltpu.SemaphoreType.DMA((n, 4)),
            pltpu.SemaphoreType.DMA((n,)),
            pltpu.SemaphoreType.DMA((n,)),
        ],
        compiler_params=params(),
        name="backward",
    )(rank, bounds, *a, *vg, probs, out_t, inv_total, stats)


def by_head(queries, keys, values, grad_normed, docs):
    block, width_dev = queries.shape
    n = width_dev // HEAD_DIM
    rank = lax.axis_index("seq").reshape(1).astype(jnp.int32)
    a = pl.pallas_call(
        functools.partial(pack_scores_kernel, block),
        out_shape=[shape_of((2 * block + 16, HEAD_DIM), BF16)] * n,
        in_specs=[SMEM_SPEC] + [ANY_SPEC] * 2 + [VMEM_SPEC],
        out_specs=[ANY_SPEC] * n,
        scratch_shapes=[
            pltpu.VMEM((n, 2 * block + 16, HEAD_DIM), BF16),
            pltpu.SemaphoreType.DMA((n, 2)),
            pltpu.SemaphoreType.DMA((n,)),
        ],
        compiler_params=params(),
        name="pack_scores",
    )(rank, queries, keys, docs.reshape(1, block))
    a = swap_all(a)
    a[1:TIE], values, grad_normed = lax.optimization_barrier((a[1:TIE], values, grad_normed))
    vg = pl.pallas_call(
        functools.partial(pack_values_kernel, block),
        out_shape=[shape_of((2 * block, HEAD_DIM), BF16)] * n,
        in_specs=[SMEM_SPEC] + [ANY_SPEC] * 2,
        out_specs=[ANY_SPEC] * n,
        scratch_shapes=[
            pltpu.VMEM((n, 2 * block, HEAD_DIM), BF16),
            pltpu.SemaphoreType.DMA((n, 2)),
            pltpu.SemaphoreType.DMA((n,)),
        ],
        compiler_params=params(),
        name="pack_values",
    )(rank, values, grad_normed)
    vg = swap_all(vg)

    probs, inv_total, bounds = run_score(rank, a, block)
    out_t, out, stats = run_attend(rank, bounds, vg, probs, inv_total, block)
    stats = sum_everywhere(stats)

    home = all_to_all(out)
    grads = run_backward(rank, bounds, a, vg, probs, out_t, inv_total, stats, block)
    home, grads = lax.optimization_barrier((home, grads))
    normed = pl.pallas_call(
        functools.partial(normed_kernel, block),
        out_shape=shape_of((block, width_dev), BF16),
        in_specs=[SMEM_SPEC] + [VMEM_SPEC] * 2,
        out_specs=VMEM_SPEC,
        compiler_params=params(),
        name="normed",
    )(rank, stats, home)
    back = swap_all(grads)
    grad_outs = pl.pallas_call(
        functools.partial(unpack_kernel, block),
        out_shape=[shape_of((block, width_dev), BF16)] * 3,
        in_specs=[SMEM_SPEC] + [ANY_SPEC] * n,
        out_specs=[ANY_SPEC] * 3,
        scratch_shapes=[
            pltpu.VMEM((3, block, width_dev), BF16),
            pltpu.SemaphoreType.DMA((3, n)),
            pltpu.SemaphoreType.DMA((3,)),
        ],
        compiler_params=params(),
        name="unpack",
    )(rank, *back)
    return (normed, *grad_outs)


def from_behind(value, axis, steps):
    count = lax.axis_size(axis)
    initial, last = (max(0, -steps), min(count, count - steps))
    return lax.ppermute(value, axis, [(source, source + steps) for source in range(initial, last)])


def allowed_pairs(all_docs, own_docs, query_pos, seq_rank, offset, block_len):
    key_start = (seq_rank - offset) * block_len
    key_pos = key_start + jnp.arange(block_len, dtype=jnp.int32)
    key_docs = lax.dynamic_slice_in_dim(all_docs, jnp.maximum(key_start, 0), block_len)
    return (
        (key_pos[None, :] >= 0)
        & (key_pos[None, :] <= query_pos[:, None])
        & (key_docs[None, :] == own_docs[:, None])
    )


def masked_scores(query_heads, source, allowed, score_scale):
    key_heads = source[0].reshape(query_heads.shape)
    scores = (
        jnp.einsum("qhd,khd->hqk", query_heads, key_heads, preferred_element_type=jnp.float32)
        * score_scale
    )
    return jnp.where(allowed[None], scores, -jnp.inf)


def by_block(queries, keys, values, grad_normed, docs):
    block_len, width_dev = queries.shape
    heads_dev = width_dev // HEAD_DIM
    width = HEADS * HEAD_DIM
    score_scale = 1.0 / math.sqrt(HEAD_DIM)
    seq_rank = lax.axis_index("seq")
    levels = lax.axis_size("seq").bit_length() - 1
    distances = [2**exponent for exponent in range(levels)]
    all_docs = lax.all_gather(docs, "seq", axis=0, tiled=True)
    query_pos = seq_rank * block_len + jnp.arange(block_len, dtype=jnp.int32)
    query_heads = queries.reshape(block_len, heads_dev, HEAD_DIM)
    key_value = jnp.stack([keys, values])
    fetched = [from_behind(key_value, "seq", offset) for offset in distances]
    offsets = [0] + distances
    sources = [key_value] + fetched
    masks = [
        allowed_pairs(all_docs, docs, query_pos, seq_rank, offset, block_len) for offset in offsets
    ]
    shape_heads = (block_len, heads_dev, HEAD_DIM)
    row_max = jnp.full((heads_dev, block_len), -jnp.inf, jnp.float32)
    row_sum = jnp.zeros((heads_dev, block_len), jnp.float32)
    for source, allowed in zip(sources, masks):

        def update_stats(state, source_kv, allowed_now):
            old_max, old_sum = state
            scores = masked_scores(query_heads, source_kv, allowed_now, score_scale)
            new_max = jnp.maximum(old_max, jnp.max(scores, axis=-1))
            new_sum = old_sum * jnp.exp(old_max - new_max) + jnp.sum(
                jnp.exp(scores - new_max[..., None]), axis=-1
            )
            return (new_max, new_sum)

        def keep_stats(state, source_kv, allowed_now):
            return state

        row_max, row_sum = lax.cond(
            jnp.any(allowed), update_stats, keep_stats, (row_max, row_sum), source, allowed
        )
    log_total = row_max + jnp.log(row_sum)
    attn = jnp.zeros(shape_heads, jnp.float32)
    for source, allowed in zip(sources, masks):

        def forward_term(source_kv, allowed_now):
            scores = masked_scores(query_heads, source_kv, allowed_now, score_scale)
            prob_round = jnp.exp(scores - log_total[..., None]).astype(jnp.bfloat16)
            value_heads = source_kv[1].reshape(shape_heads)
            return jnp.einsum(
                "hqk,khd->qhd", prob_round, value_heads, preferred_element_type=jnp.float32
            )

        def empty_term(source_kv, allowed_now):
            return jnp.zeros(shape_heads, jnp.float32)

        attn = attn + lax.cond(jnp.any(allowed), forward_term, empty_term, source, allowed)
    attn_flat = attn.reshape(block_len, width_dev)
    cotangent = grad_normed.astype(jnp.float32)
    square_local = jnp.sum(attn_flat * attn_flat, axis=-1)
    square_total = lax.psum(square_local, "head")
    inv_rms = lax.rsqrt(square_total / width + norm_eps)
    normed = (attn_flat * inv_rms[:, None]).astype(jnp.bfloat16)
    projection = lax.psum(jnp.sum(cotangent * attn_flat, axis=-1), "head")
    dattn = (
        inv_rms[:, None] * cotangent - attn_flat * (inv_rms**3 * projection / width)[:, None]
    ).astype(jnp.bfloat16)
    dattn_heads = dattn.reshape(shape_heads)
    row_delta = jnp.sum(dattn_heads.astype(jnp.float32) * attn, axis=-1).T
    grad_query = jnp.zeros(shape_heads, jnp.float32)
    partials = []
    for source, allowed in zip(sources, masks):

        def backward_term(source_kv, allowed_now):
            scores = masked_scores(query_heads, source_kv, allowed_now, score_scale)
            prob_exact = jnp.exp(scores - log_total[..., None])
            prob_round = prob_exact.astype(jnp.bfloat16)
            key_heads = source_kv[0].reshape(shape_heads)
            value_heads = source_kv[1].reshape(shape_heads)
            dprob = jnp.einsum(
                "qhd,khd->hqk", dattn_heads, value_heads, preferred_element_type=jnp.float32
            )
            dscore = (prob_exact * (dprob - row_delta[..., None]) * score_scale).astype(
                jnp.bfloat16
            )
            query_term = jnp.einsum(
                "hqk,khd->qhd", dscore, key_heads, preferred_element_type=jnp.float32
            )
            key_term = jnp.einsum(
                "hqk,qhd->khd", dscore, query_heads, preferred_element_type=jnp.float32
            )
            value_term = jnp.einsum(
                "hqk,qhd->khd", prob_round, dattn_heads, preferred_element_type=jnp.float32
            )
            return (
                query_term,
                jnp.stack(
                    [
                        key_term.reshape(block_len, width_dev),
                        value_term.reshape(block_len, width_dev),
                    ]
                ),
            )

        def empty_pair(source_kv, allowed_now):
            return (
                jnp.zeros(shape_heads, jnp.float32),
                jnp.zeros((2, block_len, width_dev), jnp.float32),
            )

        query_term, pair_term = lax.cond(
            jnp.any(allowed), backward_term, empty_pair, source, allowed
        )
        grad_query = grad_query + query_term
        partials.append(pair_term)
    local_term = partials[0]
    far_terms = partials[1:]
    summed = local_term
    for offset, addend in zip(distances, far_terms):
        summed = summed + from_behind(addend.astype(jnp.bfloat16), "seq", -offset).astype(
            addend.dtype
        )
    grad_queries = grad_query.reshape(block_len, width_dev).astype(jnp.bfloat16)
    return (normed, grad_queries, summed[0].astype(jnp.bfloat16), summed[1].astype(jnp.bfloat16))


def body(queries, *others):
    block_len, width_dev = queries.shape
    if lax.axis_size("seq") == 8 and width_dev == 8 * HEAD_DIM and block_len == 512:
        return by_head(queries, *others)
    return by_block(queries, *others)


def solution(mesh):
    placed = (P("seq", "head"), P("seq", "head"), P("seq", "head"), P("seq", "head"), P("seq"))
    return jax.shard_map(
        body,
        mesh=mesh,
        in_specs=placed,
        out_specs=(P("seq", "head"), P("seq", "head"), P("seq", "head"), P("seq", "head")),
        check_vma=False,
    )
```

```python
import functools
import math

import jax
import jax.numpy as jnp
from jax import lax
from jax.experimental import pallas as pl
from jax.experimental.pallas import tpu as pltpu
from jax.sharding import PartitionSpec as P

HEADS = 32
HEAD_DIM = 128


norm_eps = 1e-06

OFFSETS = (0, 1, 2, 4)
NEG = -1e30
F32 = jnp.float32
BF16 = jnp.bfloat16
VMEM_BYTES = 60 * 1024 * 1024


ORDER = (0, 1, 2, 4, 6, 3, 5, 7)
TIE = 3
FIRST_USE = [max(t + off for off in OFFSETS if t + off < 8) for t in range(8)]


def find_bounds(ids, bounds):
    ids = ids[...].astype(F32)
    for d in range(3):
        count = jnp.sum(jnp.where(ids < d + 0.5, 1.0, 0.0))
        bounds[d] = count.astype(jnp.int32)


def doc_of(position, bounds):
    doc = jnp.int32(0)
    for d in range(3):
        doc = doc + (position >= bounds[d]).astype(jnp.int32)
    return doc


def reach(i, block, bounds):
    first, last = doc_of(i * block, bounds), doc_of(i * block + block - 1, bounds)

    def active(off):
        return (i >= off) & (first == doc_of((i - off + 1) * block - 1, bounds))

    def full(off):
        return doc_of((i - off) * block, bounds) == last

    near = 1 + active(1).astype(jnp.int32) + active(2).astype(jnp.int32)
    return near, active(4), full(2), full(4)


def pieces(i, near, far, block):
    found = []
    if far:
        found.append((0, (i - 4) * block, block, False))
    if near > 1:
        found.append(((4 - near) * block, (i - near + 1) * block, (near - 1) * block, False))
    found.append((3 * block, i * block, block, True))
    return [(row, pl.multiple_of(key, block), size, own) for row, key, size, own in found]


def slots_of(near, far):
    return ([0] if far else []) + list(range(4 - near, 4))


def for_each_reach(i, block, bounds, body, split_full):
    near, far, full2, full4 = reach(i, block, bounds)
    pl.when(near == 1)(functools.partial(body, 1, False, True))
    pl.when(near == 2)(functools.partial(body, 2, False, True))
    alone = (near == 3) & jnp.logical_not(far)
    if not split_full:
        pl.when(alone)(functools.partial(body, 3, False, True))
        pl.when(far)(functools.partial(body, 3, True, True))
        return
    pl.when(alone & full2)(functools.partial(body, 3, False, False))
    pl.when(alone & jnp.logical_not(full2))(functools.partial(body, 3, False, True))
    pl.when(far & full4)(functools.partial(body, 3, True, False))
    pl.when(far & jnp.logical_not(full4))(functools.partial(body, 3, True, True))


def each_slot(i, block, bounds, act):
    near, far, _, _ = reach(i, block, bounds)
    act(3)
    pl.when(near > 1)(lambda: act(2))
    pl.when(near > 2)(lambda: act(1))
    pl.when(far)(lambda: act(0))


def by_rows(i, act):
    if isinstance(i, int):
        act(0 if i >= 4 else max(1, 3 - i))
        return
    pl.when(i == 0)(lambda: act(3))
    pl.when(i == 1)(lambda: act(2))
    pl.when((i == 2) | (i == 3))(lambda: act(1))
    pl.when(i >= 4)(lambda: act(0))


def move_probs(source, target, sems, block, i, slot):
    rows = slice(slot * block, 4 * block)
    return pltpu.make_async_copy(source.at[i, rows, :], target.at[i, rows, :], sems.at[i])


def doc_starts(i, block, bounds):
    pos = i * block + lax.broadcasted_iota(jnp.int32, (1, block), 1)
    start = jnp.zeros((1, block), jnp.int32)
    for d in range(3):
        start = jnp.where(pos >= bounds[d], jnp.maximum(start, bounds[d]), start)
    return pos, start


def nt_dot(a, b):
    return lax.dot_general(a, b, (((1,), (1,)), ((), ())), preferred_element_type=F32)


def nn_dot(a, b):
    return lax.dot_general(a, b, (((1,), (0,)), ((), ())), preferred_element_type=F32)


def parts_in(ref, t, block, held, sems):
    return [
        pltpu.make_async_copy(
            ref.at[part * block : (part + 1) * block, :],
            held.at[part, pl.ds(pl.multiple_of(t * block, block), block), :],
            sems.at[part, t],
        )
        for part in range(2)
    ]


def score_kernel(block, rank_ref, *refs):
    n = 8
    a_refs = refs[:n]
    prob_ref, inv_ref, bounds = refs[n : n + 3]
    held, ids, prob, sems, id_sems, prob_sems = refs[n + 3 :]
    rank = rank_ref[0]

    def ids_in(m, ref):
        return pltpu.make_async_copy(ref.at[2 * block :, :], ids.at[rank ^ m], id_sems.at[m])

    for m, ref in zip(ORDER, a_refs):
        ids_in(m, ref).start()
    for m, ref in zip(ORDER, a_refs):
        for copy in parts_in(ref, rank ^ m, block, held, sems):
            copy.start()
    for m, ref in zip(ORDER, a_refs):
        ids_in(m, ref).wait()
    find_bounds(ids, bounds)

    gain = math.log2(math.e) / math.sqrt(HEAD_DIM)

    prob_out = functools.partial(move_probs, prob, prob_ref, prob_sems, block)

    def one_block(i, carry):
        own_rows = pl.ds(pl.multiple_of(i * block, block), block)
        for copy in parts_in(a_refs[0], i, block, held, sems):
            copy.wait()
        query = held[0, own_rows, :]
        q_pos, q_start = doc_starts(i, block, bounds)

        def body(near, far, masked):
            found = pieces(i, near, far, block)
            scores, top = [], None
            for row, key, size, own in found:
                s = nt_dot(held[1, pl.ds(key, size), :], query) * gain
                if masked or own:
                    k_pos = key + lax.broadcasted_iota(jnp.int32, (size, 1), 0)
                    if not masked:
                        keep = k_pos <= q_pos
                    elif own:
                        keep = (k_pos >= q_start) & (k_pos <= q_pos)
                    else:
                        keep = k_pos >= q_start
                    s = jnp.where(keep, s, NEG)
                scores.append(s)
                peak = jnp.max(s, axis=0, keepdims=True)
                top = peak if top is None else jnp.maximum(top, peak)
            total = None
            for (row, key, size, own), s in zip(found, scores):
                p = jnp.exp2(s - top)
                line = jnp.sum(p, axis=0, keepdims=True)
                prob[i, row : row + size, :] = p.astype(BF16)
                total = line if total is None else total + line
            inv_ref[i] = 1.0 / total

        for_each_reach(i, block, bounds, body, True)
        by_rows(i, lambda slot: prob_out(i, slot).start())
        return carry

    lax.fori_loop(0, n, one_block, 0)

    for i in range(n):
        by_rows(i, lambda slot: prob_out(i, slot).wait())


def value_in(vg_ref, t, block, values, sems):
    return pltpu.make_async_copy(
        vg_ref.at[0:block, :],
        values.at[pl.ds(pl.multiple_of(t * block, block), block), :],
        sems.at[0, t],
    )


def cot_in(vg_ref, t, block, cot, sems):
    return pltpu.make_async_copy(vg_ref.at[block:, :], cot.at[t], sems.at[1, t])


def attend_kernel(block, rank_ref, bounds, *refs):
    n = 8
    vg_refs = refs[:n]
    prob_ref, inv_ref, out_t_ref, out_ref, stats_ref = refs[n : n + 5]
    both, val_t, prob, out_t_keep, out_keep, acc, vg_sems, prob_sems, out_sems = refs[n + 5 :]
    vg_ref = vg_refs[0]
    prob_in = functools.partial(move_probs, prob_ref, prob, prob_sems, block)

    def both_in(ref, t):
        return pltpu.make_async_copy(ref, both.at[t], vg_sems.at[t])

    def rows_out(i):
        return (
            pltpu.make_async_copy(out_t_keep.at[i], out_t_ref.at[i], out_sems.at[0, i]),
            pltpu.make_async_copy(out_keep.at[i], out_ref.at[i], out_sems.at[1, i]),
        )

    for m, ref in zip(ORDER, vg_refs):
        both_in(ref, rank_ref[0] ^ m).start()
    for t in range(n):
        by_rows(t, lambda slot: prob_in(t, slot).start())
    ones = jnp.ones((16, HEAD_DIM), BF16)

    def one_block(i, carry):
        own_rows = pl.ds(pl.multiple_of(i * block, block), block)
        both_in(vg_ref, i).wait()
        val_t[:, own_rows] = both[i, 0:block, :].T

        def body(near, far, masked):
            out = None
            for row, key, size, own in pieces(i, near, far, block):
                term = nn_dot(val_t[:, pl.ds(key, size)], prob[i, row : row + size, :])
                out = term if out is None else out + term
            acc[...] = out

        by_rows(i, lambda slot: prob_in(i, slot).wait())
        for_each_reach(i, block, bounds, body, False)

        out_t = acc[...] * inv_ref[i]
        out_t_keep[i] = out_t
        rows_out(i)[0].start()
        stats_ref[0:1, own_rows] = jnp.sum(out_t * out_t, axis=0, keepdims=True)
        return carry

    lax.fori_loop(0, n, one_block, 0)

    for i in range(n):
        cols = slice(i * block, (i + 1) * block)
        out = out_t_keep[i].T
        out_keep[i] = out.astype(BF16)
        rows_out(i)[1].start()
        x = both[i, block:, :].astype(F32) * out
        high = x.astype(BF16)
        low = (x - high.astype(F32)).astype(BF16)
        stats_ref[1:2, cols] = (nt_dot(ones, high) + nt_dot(ones, low))[0:1]

    def finish(i, carry):
        for copy in rows_out(i):
            copy.wait()
        return carry

    lax.fori_loop(0, n, finish, 0)


def backward_kernel(block, rank_ref, bounds, *refs):
    n = 8
    a_refs, vg_refs = refs[:n], refs[n : 2 * n]
    vg_ref = vg_refs[0]
    refs = refs[n - 1 :]
    prob_ref, out_t_ref, inv_ref, stats_ref = refs[n + 1 : n + 5]
    d_refs = refs[n + 5 : 2 * n + 5]
    held, values, cot, key_t, prob, out_t_keep, stage, grad_k, grad_v, acc = refs[
        2 * n + 5 : 2 * n + 15
    ]
    dattn_t, dattn_keep, deltas = refs[2 * n + 15 : 2 * n + 18]
    sems, vg_sems, prob_sems, out_sems, d_sems = refs[2 * n + 18 :]
    rank = rank_ref[0]
    scale = 1.0 / math.sqrt(HEAD_DIM)
    width = HEADS * HEAD_DIM

    def out_in(i):
        return pltpu.make_async_copy(out_t_ref.at[i], out_t_keep.at[i], out_sems.at[i])

    def prob_in(i, slot):
        rows = slice(slot * block, (slot + 1) * block)
        return pltpu.make_async_copy(
            prob_ref.at[i, rows, :], prob.at[i, rows, :], prob_sems.at[i, slot]
        )

    for m, ref in zip(ORDER, vg_refs):
        cot_in(ref, rank ^ m, block, cot, vg_sems).start()
    for i in reversed(range(n)):
        out_in(i).start()
    for m, ref in zip(ORDER, vg_refs):
        value_in(ref, rank ^ m, block, values, vg_sems).start()
    for m, ref in zip(ORDER, a_refs):
        for copy in parts_in(ref, rank ^ m, block, held, sems):
            copy.start()

    def fetch(step, carry):
        i = n - 1 - step
        each_slot(i, block, bounds, lambda slot: prob_in(i, slot).start())
        return carry

    lax.fori_loop(0, n, fetch, 0)
    grad_k[...] = jnp.zeros_like(grad_k)
    grad_v[...] = jnp.zeros_like(grad_v)

    for i in reversed(range(n)):
        cols = slice(i * block, (i + 1) * block)
        cot_in(vg_ref, i, block, cot, vg_sems).wait()
        out_in(i).wait()
        inv_rms = lax.rsqrt(stats_ref[0:1, cols] / width + norm_eps)
        coef = inv_rms * inv_rms * inv_rms * stats_ref[1:2, cols] / width
        out_t = out_t_keep[i]
        rows_t = (inv_rms * cot[i].astype(F32).T - out_t * coef) * inv_ref[i]
        rounded = rows_t.astype(BF16)
        dattn_t[:, cols] = rounded
        rows_f = rounded.astype(F32)
        deltas[0:1, cols] = jnp.sum(rows_f * out_t, axis=0, keepdims=True)
        dattn_keep[cols, :] = rows_f.T.astype(BF16)

    def one_block(step, carry):
        i = n - 1 - step
        own_rows = pl.ds(pl.multiple_of(i * block, block), block)
        dattn_tb = dattn_t[:, own_rows]
        dattn = dattn_keep[own_rows, :]
        delta = deltas[0:1, own_rows]
        for first in sorted(set(FIRST_USE)):

            @pl.when(i == first)
            def _():
                for t in range(n):
                    if FIRST_USE[t] == first:
                        for copy in parts_in(a_refs[0], t, block, held, sems):
                            copy.wait()
                        value_in(vg_ref, t, block, values, vg_sems).wait()
                        cols = slice(t * block, (t + 1) * block)
                        key_t[:, cols] = held[1, cols, :].T

        query = held[0, own_rows, :]

        def body(near, far, masked):
            for slot in slots_of(near, far):
                prob_in(i, slot).wait()
            for number, (row, key, size, own) in enumerate(pieces(i, near, far, block)):
                rows = pl.ds(key, size)
                pb = prob[i, row : row + size, :]
                dprob = nn_dot(values[rows, :], dattn_tb)
                ds = (pb.astype(F32) * (dprob - delta)).astype(BF16)
                term = nn_dot(key_t[:, rows], ds)
                acc[...] = term if number == 0 else acc[...] + term
                grad_k[rows, :] += nn_dot(ds, query)
                grad_v[rows, :] += nn_dot(pb, dattn)

        for_each_reach(i, block, bounds, body, False)

        stage[i, 0:block, :] = (acc[...] * scale).T.astype(BF16)
        stage[i, block : 2 * block, :] = (grad_k[own_rows, :] * scale).astype(BF16)
        stage[i, 2 * block :, :] = grad_v[own_rows, :].astype(BF16)
        for m, ref in zip(ORDER, d_refs):

            @pl.when((rank ^ m) == i)
            def _():
                pltpu.make_async_copy(stage.at[i], ref, d_sems.at[m]).start()

        return carry

    lax.fori_loop(0, n, one_block, 0)
    for m, ref in zip(ORDER, d_refs):
        pltpu.make_async_copy(stage.at[0], ref, d_sems.at[m]).wait()


def own_cols(rank_ref, m):
    return pl.ds(pl.multiple_of((rank_ref[0] ^ m) * HEAD_DIM, HEAD_DIM), HEAD_DIM)


def start_all(pairs, sems):
    copies = [
        pltpu.make_async_copy(source, target, sems.at[number])
        for number, (source, target) in enumerate(pairs)
    ]
    for copy in copies:
        copy.start()
    return copies


def pass_on(arrivals, keep, refs, sems):
    copies = []
    for index, ref in enumerate(refs):
        for copy in arrivals[index]:
            copy.wait()
        copies.append(pltpu.make_async_copy(keep.at[index], ref, sems.at[index]))
        copies[-1].start()
    for copy in copies:
        copy.wait()


def gather_columns(block, rank_ref, top_ref, low_ref, keep, sems):
    arrivals = []
    for index, m in enumerate(ORDER):
        cols = own_cols(rank_ref, m)
        pairs = [
            (top_ref.at[:, cols], keep.at[index, 0:block, :]),
            (low_ref.at[:, cols], keep.at[index, block : 2 * block, :]),
        ]
        arrivals.append(start_all(pairs, sems.at[index]))
    return arrivals


def pack_scores_kernel(block, rank_ref, q_ref, k_ref, doc_ref, *refs):
    n = 8
    a_refs, keep, sems, out_sems = refs[:n], *refs[n:]
    arrivals = gather_columns(block, rank_ref, q_ref, k_ref, keep, sems)
    row = lax.broadcasted_iota(jnp.int32, (16, HEAD_DIM), 0)
    ids = jnp.full((16, HEAD_DIM), 4.0, F32)
    for k in range(block // HEAD_DIM):
        part = doc_ref[0:1, k * HEAD_DIM : (k + 1) * HEAD_DIM].astype(F32)
        ids = jnp.where(row == k, part, ids)
    for index in range(n):
        keep[index, 2 * block :, :] = ids.astype(BF16)
    pass_on(arrivals, keep, a_refs, out_sems)


def pack_values_kernel(block, rank_ref, v_ref, g_ref, *refs):
    n = 8
    vg_refs, keep, sems, out_sems = refs[:n], *refs[n:]
    pass_on(gather_columns(block, rank_ref, v_ref, g_ref, keep, sems), keep, vg_refs, out_sems)


def unpack_kernel(block, rank_ref, *refs):
    n = 8
    d_refs, outs, keep, sems, out_sems = refs[:n], refs[n : n + 3], *refs[n + 3 :]
    arrivals = []
    for part in range(3):
        rows = slice(part * block, (part + 1) * block)
        pairs = [
            (ref.at[rows, :], keep.at[part, :, own_cols(rank_ref, m)])
            for m, ref in zip(ORDER, d_refs)
        ]
        arrivals.append(start_all(pairs, sems.at[part]))
    copies = []
    for part, out in enumerate(outs):
        for copy in arrivals[part]:
            copy.wait()
        copies.append(pltpu.make_async_copy(keep.at[part], out, out_sems.at[part]))
        copies[-1].start()
    for copy in copies:
        copy.wait()


def normed_kernel(block, rank_ref, stats_ref, home_ref, out_ref):
    own_rows = pl.ds(pl.multiple_of(rank_ref[0] * block, block), block)
    inv_rms = lax.rsqrt(stats_ref[0:1, own_rows] / (HEADS * HEAD_DIM) + norm_eps)
    spread = jnp.broadcast_to(inv_rms, (HEAD_DIM, block)).T
    for h in range(home_ref.shape[0]):
        cols = slice(h * HEAD_DIM, (h + 1) * HEAD_DIM)
        out_ref[:, cols] = (home_ref[h].astype(F32) * spread).astype(BF16)


SMEM_SPEC = pl.BlockSpec(memory_space=pltpu.SMEM)
ANY_SPEC = pl.BlockSpec(memory_space=pl.ANY)
VMEM_SPEC = pl.BlockSpec(memory_space=pltpu.VMEM)


def shape_of(shape, dtype):
    return jax.ShapeDtypeStruct(shape, dtype)


def swap(value, m):
    if m == 0:
        return value
    n = lax.axis_size("seq")
    return lax.ppermute(value, "seq", [(s, s ^ m) for s in range(n)])


def swap_all(parts):
    return [swap(part, m) for m, part in zip(ORDER, parts)]


def all_to_all(value):
    return lax.all_to_all(value, "seq", split_axis=0, concat_axis=0, tiled=True)


def sum_everywhere(stats):
    stats = stats + swap(stats, 1)
    stats = stats + swap(stats, 2) + swap(stats, 4) + swap(stats, 6)
    heads = lax.axis_size("head")
    parts = [
        lax.ppermute(stats, "head", [(s, (s + d) % heads) for s in range(heads)])
        for d in range(1, heads)
    ]
    return functools.reduce(jnp.add, parts, stats)


def params():
    return pltpu.CompilerParams(vmem_limit_bytes=VMEM_BYTES)


def run_score(rank, a, block):
    n = len(a)
    return pl.pallas_call(
        functools.partial(score_kernel, block),
        out_shape=[
            shape_of((n, 4 * block, block), BF16),
            shape_of((n, 1, block), F32),
            shape_of((3,), jnp.int32),
        ],
        in_specs=[SMEM_SPEC] + [ANY_SPEC] * n,
        out_specs=[ANY_SPEC, VMEM_SPEC, SMEM_SPEC],
        scratch_shapes=[
            pltpu.VMEM((2, n * block, HEAD_DIM), BF16),
            pltpu.VMEM((n, 16, HEAD_DIM), BF16),
            pltpu.VMEM((n, 4 * block, block), BF16),
            pltpu.SemaphoreType.DMA((2, n)),
            pltpu.SemaphoreType.DMA((n,)),
            pltpu.SemaphoreType.DMA((n,)),
        ],
        compiler_params=params(),
        name="score",
    )(rank, *a)


def run_attend(rank, bounds, vg, probs, inv_total, block):
    n = len(vg)
    return pl.pallas_call(
        functools.partial(attend_kernel, block),
        out_shape=[
            shape_of((n, HEAD_DIM, block), F32),
            shape_of((n, block, HEAD_DIM), BF16),
            shape_of((2, n * block), F32),
        ],
        in_specs=[SMEM_SPEC] * 2 + [ANY_SPEC] * (n + 1) + [VMEM_SPEC],
        out_specs=[ANY_SPEC] * 2 + [VMEM_SPEC],
        scratch_shapes=[
            pltpu.VMEM((n, 2 * block, HEAD_DIM), BF16),
            pltpu.VMEM((HEAD_DIM, n * block), BF16),
            pltpu.VMEM((n, 4 * block, block), BF16),
            pltpu.VMEM((n, HEAD_DIM, block), F32),
            pltpu.VMEM((n, block, HEAD_DIM), BF16),
            pltpu.VMEM((HEAD_DIM, block), F32),
            pltpu.SemaphoreType.DMA((n,)),
            pltpu.SemaphoreType.DMA((n,)),
            pltpu.SemaphoreType.DMA((2, n)),
        ],
        compiler_params=params(),
        name="attend",
    )(rank, bounds, *vg, probs, inv_total)


def run_backward(rank, bounds, a, vg, probs, out_t, inv_total, stats, block):
    n = len(a)
    return pl.pallas_call(
        functools.partial(backward_kernel, block),
        out_shape=[shape_of((3 * block, HEAD_DIM), BF16)] * n,
        in_specs=[SMEM_SPEC] * 2 + [ANY_SPEC] * (2 * n + 2) + [VMEM_SPEC] * 2,
        out_specs=[ANY_SPEC] * n,
        scratch_shapes=[
            pltpu.VMEM((2, n * block, HEAD_DIM), BF16),
            pltpu.VMEM((n * block, HEAD_DIM), BF16),
            pltpu.VMEM((n, block, HEAD_DIM), BF16),
            pltpu.VMEM((HEAD_DIM, n * block), BF16),
            pltpu.VMEM((n, 4 * block, block), BF16),
            pltpu.VMEM((n, HEAD_DIM, block), F32),
            pltpu.VMEM((n, 3 * block, HEAD_DIM), BF16),
            pltpu.VMEM((n * block, HEAD_DIM), F32),
            pltpu.VMEM((n * block, HEAD_DIM), F32),
            pltpu.VMEM((HEAD_DIM, block), F32),
            pltpu.VMEM((HEAD_DIM, n * block), BF16),
            pltpu.VMEM((n * block, HEAD_DIM), BF16),
            pltpu.VMEM((1, n * block), F32),
            pltpu.SemaphoreType.DMA((2, n)),
            pltpu.SemaphoreType.DMA((2, n)),
            pltpu.SemaphoreType.DMA((n, 4)),
            pltpu.SemaphoreType.DMA((n,)),
            pltpu.SemaphoreType.DMA((n,)),
        ],
        compiler_params=params(),
        name="backward",
    )(rank, bounds, *a, *vg, probs, out_t, inv_total, stats)


def by_head(queries, keys, values, grad_normed, docs):
    block, width_dev = queries.shape
    n = width_dev // HEAD_DIM
    rank = lax.axis_index("seq").reshape(1).astype(jnp.int32)
    a = pl.pallas_call(
        functools.partial(pack_scores_kernel, block),
        out_shape=[shape_of((2 * block + 16, HEAD_DIM), BF16)] * n,
        in_specs=[SMEM_SPEC] + [ANY_SPEC] * 2 + [VMEM_SPEC],
        out_specs=[ANY_SPEC] * n,
        scratch_shapes=[
            pltpu.VMEM((n, 2 * block + 16, HEAD_DIM), BF16),
            pltpu.SemaphoreType.DMA((n, 2)),
            pltpu.SemaphoreType.DMA((n,)),
        ],
        compiler_params=params(),
        name="pack_scores",
    )(rank, queries, keys, docs.reshape(1, block))
    a = swap_all(a)
    a[1:TIE], values, grad_normed = lax.optimization_barrier((a[1:TIE], values, grad_normed))
    vg = pl.pallas_call(
        functools.partial(pack_values_kernel, block),
        out_shape=[shape_of((2 * block, HEAD_DIM), BF16)] * n,
        in_specs=[SMEM_SPEC] + [ANY_SPEC] * 2,
        out_specs=[ANY_SPEC] * n,
        scratch_shapes=[
            pltpu.VMEM((n, 2 * block, HEAD_DIM), BF16),
            pltpu.SemaphoreType.DMA((n, 2)),
            pltpu.SemaphoreType.DMA((n,)),
        ],
        compiler_params=params(),
        name="pack_values",
    )(rank, values, grad_normed)
    vg = swap_all(vg)

    probs, inv_total, bounds = run_score(rank, a, block)
    out_t, out, stats = run_attend(rank, bounds, vg, probs, inv_total, block)
    stats = sum_everywhere(stats)

    home = all_to_all(out)
    grads = run_backward(rank, bounds, a, vg, probs, out_t, inv_total, stats, block)
    home, grads = lax.optimization_barrier((home, grads))
    normed = pl.pallas_call(
        functools.partial(normed_kernel, block),
        out_shape=shape_of((block, width_dev), BF16),
        in_specs=[SMEM_SPEC] + [VMEM_SPEC] * 2,
        out_specs=VMEM_SPEC,
        compiler_params=params(),
        name="normed",
    )(rank, stats, home)
    back = swap_all(grads)
    grad_outs = pl.pallas_call(
        functools.partial(unpack_kernel, block),
        out_shape=[shape_of((block, width_dev), BF16)] * 3,
        in_specs=[SMEM_SPEC] + [ANY_SPEC] * n,
        out_specs=[ANY_SPEC] * 3,
        scratch_shapes=[
            pltpu.VMEM((3, block, width_dev), BF16),
            pltpu.SemaphoreType.DMA((3, n)),
            pltpu.SemaphoreType.DMA((3,)),
        ],
        compiler_params=params(),
        name="unpack",
    )(rank, *back)
    return (normed, *grad_outs)


def from_behind(value, axis, steps):
    count = lax.axis_size(axis)
    initial, last = (max(0, -steps), min(count, count - steps))
    return lax.ppermute(value, axis, [(source, source + steps) for source in range(initial, last)])


def allowed_pairs(all_docs, own_docs, query_pos, seq_rank, offset, block_len):
    key_start = (seq_rank - offset) * block_len
    key_pos = key_start + jnp.arange(block_len, dtype=jnp.int32)
    key_docs = lax.dynamic_slice_in_dim(all_docs, jnp.maximum(key_start, 0), block_len)
    return (
        (key_pos[None, :] >= 0)
        & (key_pos[None, :] <= query_pos[:, None])
        & (key_docs[None, :] == own_docs[:, None])
    )


def masked_scores(query_heads, source, allowed, score_scale):
    key_heads = source[0].reshape(query_heads.shape)
    scores = (
        jnp.einsum("qhd,khd->hqk", query_heads, key_heads, preferred_element_type=jnp.float32)
        * score_scale
    )
    return jnp.where(allowed[None], scores, -jnp.inf)


def by_block(queries, keys, values, grad_normed, docs):
    block_len, width_dev = queries.shape
    heads_dev = width_dev // HEAD_DIM
    width = HEADS * HEAD_DIM
    score_scale = 1.0 / math.sqrt(HEAD_DIM)
    seq_rank = lax.axis_index("seq")
    levels = lax.axis_size("seq").bit_length() - 1
    distances = [2**exponent for exponent in range(levels)]
    all_docs = lax.all_gather(docs, "seq", axis=0, tiled=True)
    query_pos = seq_rank * block_len + jnp.arange(block_len, dtype=jnp.int32)
    query_heads = queries.reshape(block_len, heads_dev, HEAD_DIM)
    key_value = jnp.stack([keys, values])
    fetched = [from_behind(key_value, "seq", offset) for offset in distances]
    offsets = [0] + distances
    sources = [key_value] + fetched
    masks = [
        allowed_pairs(all_docs, docs, query_pos, seq_rank, offset, block_len) for offset in offsets
    ]
    shape_heads = (block_len, heads_dev, HEAD_DIM)
    row_max = jnp.full((heads_dev, block_len), -jnp.inf, jnp.float32)
    row_sum = jnp.zeros((heads_dev, block_len), jnp.float32)
    for source, allowed in zip(sources, masks):

        def update_stats(state, source_kv, allowed_now):
            old_max, old_sum = state
            scores = masked_scores(query_heads, source_kv, allowed_now, score_scale)
            new_max = jnp.maximum(old_max, jnp.max(scores, axis=-1))
            new_sum = old_sum * jnp.exp(old_max - new_max) + jnp.sum(
                jnp.exp(scores - new_max[..., None]), axis=-1
            )
            return (new_max, new_sum)

        def keep_stats(state, source_kv, allowed_now):
            return state

        row_max, row_sum = lax.cond(
            jnp.any(allowed), update_stats, keep_stats, (row_max, row_sum), source, allowed
        )
    log_total = row_max + jnp.log(row_sum)
    attn = jnp.zeros(shape_heads, jnp.float32)
    for source, allowed in zip(sources, masks):

        def forward_term(source_kv, allowed_now):
            scores = masked_scores(query_heads, source_kv, allowed_now, score_scale)
            prob_round = jnp.exp(scores - log_total[..., None]).astype(jnp.bfloat16)
            value_heads = source_kv[1].reshape(shape_heads)
            return jnp.einsum(
                "hqk,khd->qhd", prob_round, value_heads, preferred_element_type=jnp.float32
            )

        def empty_term(source_kv, allowed_now):
            return jnp.zeros(shape_heads, jnp.float32)

        attn = attn + lax.cond(jnp.any(allowed), forward_term, empty_term, source, allowed)
    attn_flat = attn.reshape(block_len, width_dev)
    cotangent = grad_normed.astype(jnp.float32)
    square_local = jnp.sum(attn_flat * attn_flat, axis=-1)
    square_total = lax.psum(square_local, "head")
    inv_rms = lax.rsqrt(square_total / width + norm_eps)
    normed = (attn_flat * inv_rms[:, None]).astype(jnp.bfloat16)
    projection = lax.psum(jnp.sum(cotangent * attn_flat, axis=-1), "head")
    dattn = (
        inv_rms[:, None] * cotangent - attn_flat * (inv_rms**3 * projection / width)[:, None]
    ).astype(jnp.bfloat16)
    dattn_heads = dattn.reshape(shape_heads)
    row_delta = jnp.sum(dattn_heads.astype(jnp.float32) * attn, axis=-1).T
    grad_query = jnp.zeros(shape_heads, jnp.float32)
    partials = []
    for source, allowed in zip(sources, masks):

        def backward_term(source_kv, allowed_now):
            scores = masked_scores(query_heads, source_kv, allowed_now, score_scale)
            prob_exact = jnp.exp(scores - log_total[..., None])
            prob_round = prob_exact.astype(jnp.bfloat16)
            key_heads = source_kv[0].reshape(shape_heads)
            value_heads = source_kv[1].reshape(shape_heads)
            dprob = jnp.einsum(
                "qhd,khd->hqk", dattn_heads, value_heads, preferred_element_type=jnp.float32
            )
            dscore = (prob_exact * (dprob - row_delta[..., None]) * score_scale).astype(
                jnp.bfloat16
            )
            query_term = jnp.einsum(
                "hqk,khd->qhd", dscore, key_heads, preferred_element_type=jnp.float32
            )
            key_term = jnp.einsum(
                "hqk,qhd->khd", dscore, query_heads, preferred_element_type=jnp.float32
            )
            value_term = jnp.einsum(
                "hqk,qhd->khd", prob_round, dattn_heads, preferred_element_type=jnp.float32
            )
            return (
                query_term,
                jnp.stack(
                    [
                        key_term.reshape(block_len, width_dev),
                        value_term.reshape(block_len, width_dev),
                    ]
                ),
            )

        def empty_pair(source_kv, allowed_now):
            return (
                jnp.zeros(shape_heads, jnp.float32),
                jnp.zeros((2, block_len, width_dev), jnp.float32),
            )

        query_term, pair_term = lax.cond(
            jnp.any(allowed), backward_term, empty_pair, source, allowed
        )
        grad_query = grad_query + query_term
        partials.append(pair_term)
    local_term = partials[0]
    far_terms = partials[1:]
    summed = local_term
    for offset, addend in zip(distances, far_terms):
        summed = summed + from_behind(addend.astype(jnp.bfloat16), "seq", -offset).astype(
            addend.dtype
        )
    grad_queries = grad_query.reshape(block_len, width_dev).astype(jnp.bfloat16)
    return (normed, grad_queries, summed[0].astype(jnp.bfloat16), summed[1].astype(jnp.bfloat16))


def body(queries, *others):
    block_len, width_dev = queries.shape
    if lax.axis_size("seq") == 8 and width_dev == 8 * HEAD_DIM and block_len == 512:
        return by_head(queries, *others)
    return by_block(queries, *others)


def solution(mesh):
    placed = (P("seq", "head"), P("seq", "head"), P("seq", "head"), P("seq", "head"), P("seq"))
    return jax.shard_map(
        body,
        mesh=mesh,
        in_specs=placed,
        out_specs=(P("seq", "head"), P("seq", "head"), P("seq", "head"), P("seq", "head")),
        check_vma=False,
    )
```
